512 devices in a mesh: ctx: 32 (over z, x_hi, core), ch: 16 (over y, x_lo).
Axes of the slice: x: 4 (x_hi: 2, x_lo: 2; x = x_hi * 2 + x_lo), y: 8, z: 8, core: 2. Of those that a mesh axis runs over, the one named last changes fastest.
Arguments:
- output_gate: bfloat16 [16384, 4096], P('ctx', 'ch'), may hold values from -6 to 6
- input_gate: bfloat16 [16384, 4096], P('ctx', 'ch'), may hold values from -6 to 6
- value_input: bfloat16 [16384, 4096], P('ctx', 'ch'), may hold values from -6 to 6
- short_filter: float32 [128, 4096], P(None, 'ch'), may hold values from -0.5 to 0.5
- long_filter: float32 [16384, 256], P('ctx', 'ch'), may hold values from -0.046875 to 0.046875
- skip_gain: float32 [4096], P('ch'), may hold values from -4 to 4
Outputs:
- mixed: bfloat16 [16384, 4096], P('ctx', 'ch')
The draws below stay inside these ranges and needn't reach their ends.
All inputs are finite; a program needn't handle non-finite values.
Results may differ from the reference program's by a relative error of at most 0.001.
Values may be sent and summed in bfloat16 or wider, within the bound.
A program may use at most 64 MiB of HBM per device.

```python
import math
import jax
import jax.numpy as jnp
from jax import lax

D = 4096
GROUP = 16
SHORT = 128
TOKENS = 16384
FILTERS = 256


def block_scale(key, shape, pieces, smallest, top_value):
    def one(axis_at, shards_of):
        heights = jax.random.uniform(jax.random.fold_in(jax.random.fold_in(key, 6), axis_at), (shards_of,), jnp.float32, smallest / len(pieces), top_value / len(pieces))
        return jnp.repeat(jnp.exp(heights), shape[axis_at] // shards_of).reshape((-1,) + (1,) * (len(shape) - axis_at - 1))

    gain = one(*pieces[0])
    for cut in pieces[1:]:
        gain = gain * one(*cut)
    return gain


def noise(rng, shape, deviation, reach, pieces=(), kind=jnp.bfloat16):
    values = deviation * jax.random.normal(rng, shape, jnp.float32)
    if pieces:
        values = values * block_scale(rng, shape, pieces, -0.22, 0.18)
    return jnp.clip(values, -reach, reach).astype(kind)


def setup_inputs(seed: int = 0) -> dict:
    keys = jax.random.split(jax.random.key(seed), 7)
    output_gate = noise(keys[0], (TOKENS, D), 1.0, 6.0, ((0, 32), (1, 16)))
    input_gate = noise(keys[1], (TOKENS, D), 1.0, 6.0, ((0, 32), (1, 16)))
    value_input = noise(keys[2], (TOKENS, D), 1.0, 6.0, ((0, 32), (1, 16)))
    short_filter = noise(keys[3], (SHORT, D), SHORT ** -0.5, 0.5, ((1, 16),), jnp.float32)
    long_filter = noise(keys[4], (TOKENS, FILTERS), TOKENS ** -0.5, 0.046875, ((0, 32), (1, 16)), jnp.float32)
    skip_gain = noise(keys[5], (D,), 1.0, 4.0, ((0, 16),), jnp.float32)
    return {"output_gate": output_gate, "input_gate": input_gate, "value_input": value_input, "short_filter": short_filter, "long_filter": long_filter, "skip_gain": skip_gain}


def causal_short(signal, filter_taps):
    tap_count = filter_taps.shape[0]
    length = signal.shape[0]
    padded = jnp.pad(signal, ((tap_count - 1, 0), (0, 0)))

    def add_tap(tap, total):
        start = (tap_count - 1 - tap).astype(jnp.int32)
        rows = lax.dynamic_slice_in_dim(padded, start, length, 0)
        taps = lax.dynamic_slice_in_dim(filter_taps, tap.astype(jnp.int32), 1, 0)
        return total + rows * taps

    return lax.fori_loop(0, tap_count, add_tap, jnp.zeros_like(signal))


def long_conv(gated, long_filter):
    length = gated.shape[0]
    fft_length = 2 * length
    block_count = math.gcd(long_filter.shape[1], 16)
    filter_spec = jnp.fft.rfft(long_filter, n=fft_length, axis=0)
    signal_blocks = jnp.moveaxis(gated.reshape(length, block_count, -1), 1, 0)
    filter_blocks = jnp.moveaxis(filter_spec.reshape(filter_spec.shape[0], block_count, -1), 1, 0)

    def one_block(pair):
        signal, spectrum = pair
        signal_spec = jnp.fft.rfft(signal, n=fft_length, axis=0)
        widened = jnp.repeat(spectrum, GROUP, axis=1)
        return jnp.fft.irfft(signal_spec * widened, n=fft_length, axis=0)[:length]

    result = lax.map(one_block, (signal_blocks, filter_blocks))
    return jnp.moveaxis(result, 0, 1).reshape(length, -1)


def reference(output_gate, input_gate, value_input, short_filter, long_filter, skip_gain):
    short_out = causal_short(value_input.astype(jnp.float32), short_filter)
    gated = input_gate.astype(jnp.float32) * short_out
    long_out = long_conv(gated, long_filter)
    mixed = output_gate.astype(jnp.float32) * (long_out + skip_gain[None, :] * gated)
    return mixed.astype(jnp.bfloat16)
```

```python
import functools
import math

import jax
import jax.numpy as jnp
import numpy as np
from jax import lax
from jax.experimental import pallas as pl
from jax.experimental.pallas import tpu as pltpu
from jax.sharding import PartitionSpec as P

LANES = 128
OWN = 8
HALF = 4
F32 = jnp.float32
BF16 = jnp.bfloat16


def split_np(table):
    high = table.astype(BF16)
    low = (table - high.astype(np.float32)).astype(BF16)
    return high, low


def tables(rows):
    length = rows * LANES
    n1 = np.arange(rows)
    n2 = np.arange(LANES)
    first = np.pi * n1[None, :] * LANES / (2 * length) - 2 * np.pi * ((n1[:, None] * n1[None, :]) % rows) / rows
    twist = np.pi * n2[None, :] / (2 * length) - 2 * np.pi * ((n1[:, None] * n2[None, :]) % length) / length
    second = -2 * np.pi * ((n2[:, None] * n2[None, :]) % LANES) / LANES
    col = np.concatenate([np.cos(first), np.sin(first)], 0).astype(np.float32)
    col_hi, col_lo = split_np(col)
    col_fwd = np.concatenate([col_hi, col_hi, col_lo], 1)
    back = np.concatenate([np.cos(first).T, np.sin(first).T], 1).astype(np.float32)
    back_hi, back_lo = split_np(back)
    col_inv = np.concatenate([back_hi, back_lo], 0)
    cos2, sin2 = np.cos(second), np.sin(second)
    row = np.block([[cos2, sin2], [-sin2, cos2]]).astype(np.float32)
    row_fwd = np.concatenate(split_np(row), 0)
    row_inv = np.concatenate(split_np(np.ascontiguousarray(row.T)), 0)
    turn = np.concatenate([np.cos(twist), np.sin(twist)], 0).astype(np.float32)
    return col_fwd, col_inv, row_fwd, row_inv, turn


def mm(a, b):
    return jnp.dot(a, b, preferred_element_type=F32)


def halves(x):
    high = x.astype(BF16)
    return high, (x - high.astype(F32)).astype(BF16)


def kernel(
    geometry,
    og_any, ig_any, vi_any, sf_any, lf_any, skip_any, colf_any, coli_any, rowf_any, rowi_any, turn_any,
    out_any,
    og, ig, vi, sf, lf, skip, colf, coli, rowf, rowi, turn,
    fsend, frecv, msend, mrecv, rsend, rrecv,
    sft, toep, fil, spec, both, gate, keep, fin, outv,
    in_sem, fs_sem, fr_sem, ms_sem, mr_sem, rs_sem, rr_sem, out_sem,
):
    n_z, n_x, n_core = geometry
    n_dev = n_z * n_x * n_core
    me = lax.axis_index("ctx")
    my_z = me // (n_x * n_core)
    my_in = me % (n_x * n_core)
    my_core = me % n_core
    tokens, chans = vi.shape
    q_count = tokens // LANES
    rows = n_dev * q_count

    def peer(j):
        m = j // (n_x * n_core)
        r = (n_x * n_core) - 1 - j % (n_x * n_core)
        step = (m // 2 + 1) * (1 - 2 * ((m + my_core) % 2))
        last = m == n_z - 1
        step = jnp.where(last, 0, step)
        z = (my_z + step + n_z) % n_z
        inner = (my_in + r) % (n_x * n_core)
        return z * (n_x * n_core) + inner

    barrier = pltpu.get_barrier_semaphore()

    def hello(j, _):
        pl.semaphore_signal(barrier, inc=1, device_id={"ctx": peer(j)}, device_id_type=pl.DeviceIdType.MESH)
        return 0

    lax.fori_loop(0, n_dev - 1, hello, 0)

    loads = [
        pltpu.make_async_copy(src, dst, in_sem.at[i])
        for i, (src, dst) in enumerate(
            [
                (vi_any, vi), (ig_any, ig), (lf_any, lf), (og_any, og), (sf_any, sf), (skip_any, skip),
                (colf_any, colf), (coli_any, coli), (rowf_any, rowf), (rowi_any, rowi), (turn_any, turn),
            ]
        )
    ]
    for copy in loads:
        copy.start()

    def send_all(src, dst, ssem, rsem):
        pltpu.make_async_copy(src.at[me], dst.at[me], rsem).start()

        def go(j, _):
            p = peer(j)
            pltpu.make_async_remote_copy(
                src_ref=src.at[p],
                dst_ref=dst.at[me],
                send_sem=ssem,
                recv_sem=rsem,
                device_id={"ctx": p},
                device_id_type=pl.DeviceIdType.MESH,
            ).start()
            return 0

        lax.fori_loop(0, n_dev - 1, go, 0)

    def arrived(ref, sem):
        pltpu.make_async_copy(ref, ref, sem).wait()

    sub = lax.broadcasted_iota(jnp.int32, (LANES, LANES), 0) % OWN < HALF
    blocks = chans // LANES
    per_block = LANES // OWN

    def pick(a, b, second):
        if second:
            return jnp.where(sub, pltpu.roll(a, LANES - HALF, 0), b)
        return jnp.where(sub, a, pltpu.roll(b, HALF, 0))

    loads[2].wait()
    group = lax.broadcasted_iota(jnp.int32, (LANES, LANES), 0)
    del group
    for g in range(n_dev // 2):
        for q in range(q_count):
            row = lf[pl.ds(g, 1), q * LANES : (q + 1) * LANES]
            fsend[2 * g, pl.ds(q, 1), :] = row
            fsend[2 * g + 1, pl.ds(q, 1), :] = row

    loads[0].wait()
    loads[1].wait()
    loads[3].wait()
    for b in range(blocks):
        lanes = slice(b * LANES, (b + 1) * LANES)
        dests = slice(b * per_block, (b + 1) * per_block)
        for half in range(2):
            mixed = []
            gates = []
            for q in range(q_count):
                toks = slice(q * LANES, (q + 1) * LANES)
                v = vi[toks, lanes].astype(F32).T
                i = ig[toks, lanes].astype(F32).T
                gates.append(og[toks, lanes].astype(F32).T)
                mixed.append(pick(v, i, half).reshape(per_block, OWN, LANES))
            pairs = [
                pick(gates[q], gates[q + 1], half).reshape(per_block, OWN, LANES) for q in range(0, q_count, 2)
            ]
            packed = mixed + pairs
            for k in range(0, len(packed), 2):
                tile = jnp.concatenate([packed[k], packed[k + 1]], axis=1).astype(BF16)
                msend[half, dests, k * OWN : (k + 2) * OWN, :] = tile

    pl.semaphore_wait(barrier, n_dev - 1)
    send_all(fsend, frecv, fs_sem, fr_sem)
    for half in range(2):
        send_all(msend.at[half], mrecv.at[half], ms_sem.at[half], mr_sem.at[half])

    loads[4].wait()
    for b in range(blocks):
        sft[b * LANES : (b + 1) * LANES, :] = sf[:, b * LANES : (b + 1) * LANES].T
    taps8 = sft[pl.ds(pl.multiple_of(OWN * me, OWN), OWN), :]
    above = lax.broadcasted_iota(jnp.int32, (LANES, LANES), 1) >= lax.broadcasted_iota(jnp.int32, (LANES, LANES), 0)
    for c in range(OWN):
        row = jnp.broadcast_to(taps8[c : c + 1, :], (LANES, LANES))
        turned = pltpu.roll(row, 0, 1, stride=1, stride_axis=0)
        high, low = halves(turned)
        zero = jnp.zeros((LANES, LANES), BF16)
        toep[c, 0:LANES, 0:LANES] = jnp.where(above, high, zero)
        toep[c, LANES:, 0:LANES] = jnp.where(above, zero, high)
        toep[c, 0:LANES, LANES:] = jnp.where(above, low, zero)
        toep[c, LANES:, LANES:] = jnp.where(above, zero, low)

    for i in (5, 6, 7, 8, 9, 10):
        loads[i].wait()
    turn_re = turn[0:rows, :]
    turn_im = turn[rows:, :]

    def forward(block):
        high, low = halves(block)
        both_hl = jnp.concatenate([high, low], axis=0)
        first = mm(colf[:, 0 : 2 * rows], both_hl) + mm(colf[:, 2 * rows :], high)
        parts = []
        for k in range(block.shape[1] // LANES):
            re = first[0:rows, k * LANES : (k + 1) * LANES]
            im = first[rows:, k * LANES : (k + 1) * LANES]
            parts.append(jnp.concatenate([re * turn_re - im * turn_im, re * turn_im + im * turn_re], axis=1))
        return parts

    def along(block, table):
        high, low = halves(block)
        main = table[0 : 2 * LANES, :]
        return mm(high, main) + mm(low, main) + mm(high, table[2 * LANES :, :])

    arrived(frecv, fr_sem)
    for s in range(n_dev):
        fil[q_count * s : q_count * (s + 1), :] = frecv[s]
    scale = 1.0 / (rows * LANES)
    spec[...] = along(forward(fil[...])[0], rowf) * scale

    for half in range(2):
        arrived(mrecv.at[half], mr_sem.at[half])
        data = mrecv[half]
        main = q_count * OWN
        both[...] = data[:, 0:main, :].astype(F32).reshape(rows * OWN, LANES)
        gate[...] = data[:, main:, :].astype(F32).reshape(rows * HALF, LANES)
        spectra = []
        for pair in range(2):
            gated = []
            for c in (2 * pair, 2 * pair + 1):
                v = both[pl.ds(c, rows, stride=OWN), :]
                i = both[pl.ds(HALF + c, rows, stride=OWN), :]
                line = lax.broadcasted_iota(jnp.int32, (rows, LANES), 0)
                before = jnp.where(line == 0, 0.0, pltpu.roll(v, 1, 0))
                taken = jnp.concatenate([v.astype(BF16), before.astype(BF16)], axis=1)
                short = mm(taken, toep[half * HALF + c])
                gated.append(i * (short[:, 0:LANES] + short[:, LANES:]))
            block = jnp.concatenate(gated, axis=1)
            keep[pair] = block
            spectra += forward(block)
        stacked = along(jnp.concatenate(spectra, axis=0), rowf)
        prods = []
        h_re = spec[:, 0:LANES]
        h_im = spec[:, LANES:]
        for c in range(HALF):
            re = stacked[c * rows : (c + 1) * rows, 0:LANES]
            im = stacked[c * rows : (c + 1) * rows, LANES:]
            prods.append(jnp.concatenate([re * h_re - im * h_im, re * h_im + im * h_re], axis=1))
        back = along(jnp.concatenate(prods, axis=0), rowi)
        for pair in range(2):
            reals = []
            imags = []
            for c in (2 * pair, 2 * pair + 1):
                re = back[c * rows : (c + 1) * rows, 0:LANES]
                im = back[c * rows : (c + 1) * rows, LANES:]
                reals.append(re * turn_re + im * turn_im)
                imags.append(im * turn_re - re * turn_im)
            block = jnp.concatenate([jnp.concatenate(reals, axis=1), jnp.concatenate(imags, axis=1)], axis=0)
            high, low = halves(block)
            wide = mm(coli[...], high)
            result = wide[0:rows] + wide[rows:] + mm(coli[0:rows, :], low)
            for k in range(2):
                c = 2 * pair + k
                lanes = slice(k * LANES, (k + 1) * LANES)
                gain = skip[half * HALF + c + OWN * me]
                total = result[:, lanes] + gain * keep[pair, :, lanes]
                fin[pl.ds(c, rows, stride=HALF), :] = gate[pl.ds(c, rows, stride=HALF), :] * total
        rsend[half] = fin[...].reshape(n_dev, q_count * HALF, LANES).astype(BF16)
        send_all(rsend.at[half], rrecv.at[half], rs_sem.at[half], rr_sem.at[half])

    arrived(rrecv.at[0], rr_sem.at[0])
    arrived(rrecv.at[1], rr_sem.at[1])
    for b in range(blocks):
        dests = slice(b * per_block, (b + 1) * per_block)
        lanes = slice(b * LANES, (b + 1) * LANES)
        first = rrecv[0, dests].astype(F32)
        second = rrecv[1, dests].astype(F32)
        for k in range(q_count // 2):
            a = first[:, k * OWN : (k + 1) * OWN, :].reshape(LANES, LANES)
            c = second[:, k * OWN : (k + 1) * OWN, :].reshape(LANES, LANES)
            outv[2 * k * LANES : (2 * k + 1) * LANES, lanes] = pick(a, c, 0).T.astype(BF16)
            outv[(2 * k + 1) * LANES : (2 * k + 2) * LANES, lanes] = pick(a, c, 1).T.astype(BF16)
    done = pltpu.make_async_copy(outv, out_any, out_sem)
    done.start()
    sent = n_dev - 1
    arrived(fsend.at[pl.ds(0, sent)], fs_sem)
    for half in range(2):
        arrived(msend.at[half, pl.ds(0, sent)], ms_sem.at[half])
        arrived(rsend.at[half, pl.ds(0, sent)], rs_sem.at[half])
    done.wait()


def local(geometry, output_gate, input_gate, value_input, short_filter, long_filter, skip_gain):
    n_dev = math.prod(geometry)
    tokens, chans = value_input.shape
    q_count = tokens // LANES
    rows = n_dev * q_count
    tabs = [jnp.asarray(t) for t in tables(rows)]
    operands = [output_gate, input_gate, value_input, short_filter, long_filter.T, skip_gain] + tabs
    message = q_count * (OWN + HALF)
    scratch = [pltpu.VMEM(x.shape, x.dtype) for x in operands]
    scratch[5] = pltpu.SMEM(skip_gain.shape, F32)
    scratch += [
        pltpu.VMEM((n_dev, q_count, LANES), F32),
        pltpu.VMEM((n_dev, q_count, LANES), F32),
        pltpu.VMEM((2, n_dev, message, LANES), BF16),
        pltpu.VMEM((2, n_dev, message, LANES), BF16),
        pltpu.VMEM((2, n_dev, q_count * HALF, LANES), BF16),
        pltpu.VMEM((2, n_dev, q_count * HALF, LANES), BF16),
        pltpu.VMEM((chans, LANES), F32),
        pltpu.VMEM((OWN, 2 * LANES, 2 * LANES), BF16),
        pltpu.VMEM((rows, LANES), F32),
        pltpu.VMEM((rows, 2 * LANES), F32),
        pltpu.VMEM((rows * OWN, LANES), F32),
        pltpu.VMEM((rows * HALF, LANES), F32),
        pltpu.VMEM((2, rows, 2 * LANES), F32),
        pltpu.VMEM((rows * HALF, LANES), F32),
        pltpu.VMEM((tokens, chans), BF16),
        pltpu.SemaphoreType.DMA((len(operands),)),
        pltpu.SemaphoreType.DMA,
        pltpu.SemaphoreType.DMA,
        pltpu.SemaphoreType.DMA((2,)),
        pltpu.SemaphoreType.DMA((2,)),
        pltpu.SemaphoreType.DMA((2,)),
        pltpu.SemaphoreType.DMA((2,)),
        pltpu.SemaphoreType.DMA,
    ]
    return pl.pallas_call(
        functools.partial(kernel, geometry),
        out_shape=jax.ShapeDtypeStruct((tokens, chans), BF16),
        in_specs=[pl.BlockSpec(memory_space=pl.ANY)] * len(operands),
        out_specs=pl.BlockSpec(memory_space=pl.ANY),
        scratch_shapes=scratch,
        compiler_params=pltpu.CompilerParams(collective_id=0, has_side_effects=True, vmem_limit_bytes=48 << 20),
    )(*operands)


def solution(mesh):
    placed = (
        P("ctx", "ch"),
        P("ctx", "ch"),
        P("ctx", "ch"),
        P(None, "ch"),
        P("ctx", "ch"),
        P("ch"),
    )
    n_ctx = mesh.shape["ctx"]
    geometry = (n_ctx // 4, 2, 2)
    return jax.shard_map(
        functools.partial(local, geometry), mesh=mesh, in_specs=placed, out_specs=P("ctx", "ch"), check_vma=False
    )
```

```python
import functools
import math

import jax
import jax.numpy as jnp
import numpy as np
from jax import lax
from jax.experimental import pallas as pl
from jax.experimental.pallas import tpu as pltpu
from jax.sharding import PartitionSpec as P

LANES = 128
OWN = 8
INNER = 4
F32 = jnp.float32
BF16 = jnp.bfloat16
MESH = pl.DeviceIdType.MESH
KNEE = 64.0
SPAN = 120.0
POWER = 2 * SPAN / math.log2(1 + KNEE)


def split_np(table):
    table = table.astype(np.float32)
    high = table.astype(BF16)
    low = (table - high.astype(np.float32)).astype(BF16)
    return high, low


def long_tables(rows):
    length = rows * LANES
    n1 = np.arange(rows)
    n2 = np.arange(LANES)
    first = np.pi * n1[None, :] * LANES / (2 * length) - 2 * np.pi * ((n1[:, None] * n1[None, :]) % rows) / rows
    twist = np.pi * n2[None, :] / (2 * length) - 2 * np.pi * ((n1[:, None] * n2[None, :]) % length) / length
    second = -2 * np.pi * ((n2[:, None] * n2[None, :]) % LANES) / LANES
    hi, lo = split_np(np.concatenate([np.cos(first), np.sin(first)], 0))
    col_fwd = np.concatenate([hi, hi, lo], 1)
    cos1, sin1 = np.cos(first).T, np.sin(first).T
    hi, lo = split_np(np.block([[cos1, sin1], [-sin1, cos1]]))
    col_inv = np.concatenate([hi, hi, lo], 1)
    cos2, sin2 = np.cos(second), np.sin(second)
    row = np.block([[cos2, sin2], [-sin2, cos2]])
    row_fwd = np.concatenate(split_np(row), 0)
    row_inv = np.concatenate(split_np(row.T), 0)
    turn = np.concatenate([np.cos(twist), np.sin(twist)], 0).astype(np.float32)
    return col_fwd, col_inv, row_fwd, row_inv, turn


def short_tables():
    size = 2 * LANES
    n = np.arange(size)
    k = np.arange(LANES)
    angle = 2 * np.pi * ((n[:, None] * k[None, :]) % size) / size
    re, im = np.cos(angle), -np.sin(angle)
    im[:, 0] = np.where(n % 2 == 0, 1.0, -1.0)
    fwd = np.concatenate(split_np(np.concatenate([re, im], 1)), 0)
    weight = np.where(k == 0, 1.0, 2.0) / size
    back = np.concatenate([(re * weight).T, (im * weight).T], 0)[:, LANES:]
    inv = np.concatenate(split_np(back), 1)
    return fwd, inv


def mm(a, b):
    return jnp.dot(a, b, preferred_element_type=F32)


def halves(x):
    high = x.astype(BF16)
    return high, (x - high.astype(F32)).astype(BF16)


def peak(x):
    top = jnp.max(jnp.max(jnp.abs(x), axis=0, keepdims=True), axis=1, keepdims=True)
    return jnp.broadcast_to(jnp.maximum(top, 1e-30), (1, LANES))


def encode(x, top):
    size = jnp.exp2(POWER * jnp.log2(1.0 + jnp.abs(x) * (KNEE / top)) - SPAN)
    return jnp.where(x < 0, -size, size)


def decode(code, top):
    size = (jnp.exp2((jnp.log2(jnp.abs(code)) + SPAN) * (1.0 / POWER)) - 1.0) * (top * (1.0 / KNEE))
    return jnp.where(code < 0, -size, size)


def along(block, table):
    high, low = halves(block)
    main = table[0 : 2 * LANES, :]
    return mm(high, main) + mm(low, main) + mm(high, table[2 * LANES :, :])


def kernel(
    n_z,
    og_any, ig_any, vi_any, sf_any, lf_any, skip_any, colf_any, coli_any, rowf_any, rowi_any, turn_any, shf_any, shi_any,
    out_any,
    og, ig, vi, sf, lf, skip, colf, coli, rowf, rowi, turn, shf, shi,
    halo, vt, igt, skipt, taps, keep, fsend, frecv, msend, mrecv, tsend, trecv, rsend, rrecv, usend, urecv,
    spec, xs, cross, carry, fin, outv,
    in_sem, halo_sem, fs_sem, fr_sem, ms_sem, mr_sem, ts_sem, tr_sem, rs_sem, rr_sem, us_sem, ur_sem, out_sem,
):
    n_dev = n_z * INNER
    half_z = n_z // 2
    half_dev = n_dev // 2
    me = lax.axis_index("ctx")
    my_z = me // INNER
    my_in = me % INNER
    my_core = me % 2
    my_half = me // half_dev
    tokens, chans = vi.shape
    q_count = tokens // LANES
    rows = half_dev * q_count
    blocks = chans // LANES
    per_block = LANES // OWN

    inners = [(my_in + r) % INNER for r in range(INNER)]
    turns = []
    for d in range(1, n_z // 2):
        turns += [d, -d]
    turns += [n_z // 2, 0]
    sign = 1 - 2 * my_core
    planes = [((my_z + sign * d + n_z) % n_z) * INNER for d in turns]
    peers = [z + i for z in planes for i in inners[1:] + inners[:1]][:-1]

    barrier = pltpu.get_barrier_semaphore()
    for p in peers:
        pl.semaphore_signal(barrier, inc=1, device_id={"ctx": p}, device_id_type=MESH)

    order = [
        (vi_any, vi), (ig_any, ig), (shf_any, shf), (sf_any, sf), (lf_any, lf), (shi_any, shi), (og_any, og), (skip_any, skip),
        (colf_any, colf), (coli_any, coli), (rowf_any, rowf), (rowi_any, rowi), (turn_any, turn),
    ]
    loads = [pltpu.make_async_copy(src, dst, in_sem.at[i]) for i, (src, dst) in enumerate(order)]
    for copy in loads:
        copy.start()

    def remote(src, dst, ssem, rsem, p):
        pltpu.make_async_remote_copy(
            src_ref=src, dst_ref=dst, send_sem=ssem, recv_sem=rsem, device_id={"ctx": p}, device_id_type=MESH
        ).start()

    def arrived(ref, sem):
        pltpu.make_async_copy(ref, ref, sem).wait()

    def send_all(src_of, dst, ssem, rsem):
        pltpu.make_async_copy(src_of(me), dst.at[me], rsem).start()
        for p in peers:
            remote(src_of(p), dst.at[me], ssem, rsem, p)

    def put_block(b, q):
        toks = slice(q * LANES, (q + 1) * LANES)
        lanes = slice(b * LANES, (b + 1) * LANES)
        vt[q + 1, lanes, :] = vi[toks, lanes].astype(F32).T.astype(BF16)
        igt[q, lanes, :] = ig[toks, lanes].astype(F32).T

    loads[0].wait()
    loads[1].wait()
    for q in range(q_count):
        for b in range(blocks):
            put_block(b, q)

    loads[2].wait()
    loads[3].wait()
    lane = lax.broadcasted_iota(jnp.int32, (LANES, LANES), 1)
    for b in range(blocks):
        lanes = slice(b * LANES, (b + 1) * LANES)
        high, low = halves(sf[:, lanes].T)
        upper = shf[0:LANES, :]
        freq = mm(high, upper) + mm(low, upper) + mm(high, shf[2 * LANES : 3 * LANES, :])
        f_re, f_im = freq[:, 0:LANES], freq[:, LANES:]
        taps[0, lanes, :] = f_re
        taps[1, lanes, :] = jnp.where(lane == 0, 0.0, f_im)
        taps[2, lanes, :] = jnp.where(lane == 0, f_im, f_re)

    loads[4].wait()
    for g in range(n_dev // 2):
        for q in range(q_count):
            fsend[g, pl.ds(q, 1), :] = lf[pl.ds(g, 1), q * LANES : (q + 1) * LANES]
    loads[5].wait()

    def short(q):
        for b in range(blocks):
            lanes = slice(b * LANES, (b + 1) * LANES)
            window = jnp.concatenate([vt[q, lanes, :], vt[q + 1, lanes, :]], axis=1)
            freq = mm(window, shf[0 : 2 * LANES, :]) + mm(window, shf[2 * LANES :, :])
            re, im = freq[:, 0:LANES], freq[:, LANES:]
            f_re, f_zero, f_top = taps[0, lanes, :], taps[1, lanes, :], taps[2, lanes, :]
            prod = jnp.concatenate([re * f_re - im * f_zero, re * f_zero + im * f_top], axis=1)
            high, low = halves(prod)
            wide = mm(high, shi[...])
            keep[q, lanes, :] = igt[q, lanes, :] * (wide[:, 0:LANES] + wide[:, LANES:] + mm(low, shi[:, 0:LANES]))

    def pack(part):
        q = 2 * part
        top = peak(keep[q : q + 2].reshape(2 * chans, LANES))
        tsend[part] = top
        first = encode(keep[q], top).reshape(n_dev, OWN, LANES)
        second = encode(keep[q + 1], top).reshape(n_dev, OWN, LANES)
        msend[part] = jnp.concatenate([first, second], axis=1).astype(BF16)

    parts = q_count // 2
    for q in range(q_count - 1, 0, -1):
        short(q)
    for part in range(parts - 1, 0, -1):
        pack(part)

    pl.semaphore_wait(barrier, n_dev - 1)
    remote(vi.at[tokens - LANES :, :], halo, halo_sem.at[0], halo_sem.at[1], (me + 1) % n_dev)
    send_all(lambda p: fsend.at[p // 2], frecv, fs_sem, fr_sem)

    def send_part(part):
        send_all(lambda p: msend.at[part, p], mrecv.at[part], ms_sem.at[part], mr_sem.at[part, my_half])
        send_all(lambda p: tsend.at[part], trecv.at[part], ts_sem.at[part], tr_sem.at[part, my_half])

    for part in range(parts - 1, 0, -1):
        send_part(part)

    pltpu.make_async_copy(halo, halo, halo_sem.at[1]).wait()
    for b in range(blocks):
        lanes = slice(b * LANES, (b + 1) * LANES)
        before = halo[:, lanes].astype(F32).T
        vt[0, lanes, :] = jnp.where(me > 0, before, 0.0).astype(BF16)
    short(0)
    pack(0)
    send_part(0)

    for i in range(6, len(order)):
        loads[i].wait()
    for b in range(blocks):
        lanes = slice(b * LANES, (b + 1) * LANES)
        skipt[lanes, :] = jnp.broadcast_to(skip[:, lanes], (LANES, LANES)).T

    turn_re = turn[0:rows, :]
    turn_im = turn[rows:, :]

    def forward(block):
        high, low = halves(block)
        first = mm(colf[...], jnp.concatenate([high, low, high], axis=0))
        pieces = []
        for k in range(block.shape[1] // LANES):
            re = first[0:rows, k * LANES : (k + 1) * LANES]
            im = first[rows:, k * LANES : (k + 1) * LANES]
            pieces.append(jnp.concatenate([re * turn_re - im * turn_im, re * turn_im + im * turn_re], axis=1))
        return along(jnp.concatenate(pieces, axis=0), rowf[...])

    def backward(block, keep_rows):
        mid = along(block, rowi[...])
        reals, imags = [], []
        for c in range(OWN):
            re = mid[c * rows : (c + 1) * rows, 0:LANES]
            im = mid[c * rows : (c + 1) * rows, LANES:]
            reals.append(re * turn_re + im * turn_im)
            imags.append(im * turn_re - re * turn_im)
        high, low = halves(jnp.concatenate([jnp.concatenate(reals, axis=1), jnp.concatenate(imags, axis=1)], axis=0))
        return mm(coli[0:keep_rows, :], jnp.concatenate([high, low, high], axis=0))

    def times(spectra, which):
        h_re = spec[which, :, 0:LANES]
        h_im = spec[which, :, LANES:]
        out = []
        for c in range(OWN):
            re = spectra[c * rows : (c + 1) * rows, 0:LANES]
            im = spectra[c * rows : (c + 1) * rows, LANES:]
            out.append(jnp.concatenate([re * h_re - im * h_im, re * h_im + im * h_re], axis=1))
        return jnp.concatenate(out, axis=0)

    arrived(frecv, fr_sem)
    for s in range(n_dev):
        which, at = s // half_dev, s % half_dev
        fin[q_count * at : q_count * (at + 1), which * LANES : (which + 1) * LANES] = frecv[s]
    both = forward(fin[...]) * (1.0 / (rows * LANES))
    spec[0] = both[0:rows]
    spec[1] = both[rows:]

    def owned(half):
        span = pl.ds(half * half_dev, half_dev)
        got = []
        for part in range(parts):
            arrived(mrecv.at[part, span], mr_sem.at[part, half])
            arrived(trecv.at[part, span], tr_sem.at[part, half])
            got.append(decode(mrecv[part, span].astype(F32), trecv[part, span]))
        xs[...] = jnp.concatenate(got, axis=1).reshape(rows * OWN, LANES)
        return jnp.concatenate([xs[pl.ds(c, rows, stride=OWN), :] for c in range(OWN)], axis=1)

    def give_back(half, result):
        top = peak(result)
        usend[half] = top
        wide = jnp.concatenate([top] * OWN, axis=1)
        code = encode(result, wide)
        for c in range(OWN):
            xs[pl.ds(c, rows, stride=OWN), :] = code[:, c * LANES : (c + 1) * LANES]
        rsend[half] = xs[...].reshape(half_dev, q_count * OWN, LANES).astype(BF16)
        for k in range(half_z):
            z = (my_z + k) % half_z
            for r in range(INNER):
                at = z * INNER + inners[r]
                p = half * half_dev + at

                def away():
                    remote(rsend.at[half, at], rrecv.at[me], rs_sem, rr_sem, p)
                    remote(usend.at[half], urecv.at[me], us_sem, ur_sem, p)

                if k or r:
                    away()
                else:
                    pl.when(my_half != half)(away)

                    @pl.when(my_half == half)
                    def _():
                        pltpu.make_async_copy(rsend.at[half, at], rrecv.at[me], rr_sem).start()
                        pltpu.make_async_copy(usend.at[half], urecv.at[me], ur_sem).start()

    spectra = forward(owned(0))
    result = backward(times(spectra, 0), 2 * rows)
    carry[...] = result[rows:]
    give_back(0, result[0:rows])
    cross[...] = times(spectra, 1)
    spectra = forward(owned(1))
    give_back(1, backward(times(spectra, 0) + cross[...], rows) + carry[...])

    arrived(rrecv, rr_sem)
    arrived(urecv, ur_sem)
    for q in range(q_count):
        toks = slice(q * LANES, (q + 1) * LANES)
        code = rrecv[:, (q // 2) * 2 * OWN : (q // 2 + 1) * 2 * OWN, :].astype(F32)[:, (q % 2) * OWN : (q % 2 + 1) * OWN, :]
        total = decode(code, urecv[...]).reshape(chans, LANES) + skipt[...] * keep[q]
        for b in range(blocks):
            lanes = slice(b * LANES, (b + 1) * LANES)
            outv[toks, lanes] = (og[toks, lanes].astype(F32) * total[lanes, :].T).astype(BF16)
    done = pltpu.make_async_copy(outv, out_any, out_sem)
    done.start()

    sent = pl.ds(0, n_dev - 1)
    arrived(halo, halo_sem.at[0])
    arrived(frecv.at[sent], fs_sem)
    for part in range(parts):
        arrived(mrecv.at[part, sent], ms_sem.at[part])
        arrived(trecv.at[part, sent], ts_sem.at[part])
    arrived(rrecv.at[sent], rs_sem)
    arrived(urecv.at[sent], us_sem)
    done.wait()


def local(n_z, output_gate, input_gate, value_input, short_filter, long_filter, skip_gain):
    n_dev = n_z * INNER
    tokens, chans = value_input.shape
    q_count = tokens // LANES
    parts = q_count // 2
    rows = n_dev * q_count // 2
    tabs = [jnp.asarray(t) for t in long_tables(rows) + short_tables()]
    operands = [output_gate, input_gate, value_input, short_filter, long_filter.T, skip_gain.reshape(1, chans)] + tabs
    dma = pltpu.SemaphoreType.DMA
    scratch = [pltpu.VMEM(x.shape, x.dtype) for x in operands]
    scratch += [
        pltpu.VMEM((LANES, chans), BF16),
        pltpu.VMEM((q_count + 1, chans, LANES), BF16),
        pltpu.VMEM((q_count, chans, LANES), F32),
        pltpu.VMEM((chans, LANES), F32),
        pltpu.VMEM((3, chans, LANES), F32),
        pltpu.VMEM((q_count, chans, LANES), F32),
        pltpu.VMEM((n_dev // 2, q_count, LANES), F32),
        pltpu.VMEM((n_dev, q_count, LANES), F32),
        pltpu.VMEM((parts, n_dev, 2 * OWN, LANES), BF16),
        pltpu.VMEM((parts, n_dev, 2 * OWN, LANES), BF16),
        pltpu.VMEM((parts, 1, LANES), F32),
        pltpu.VMEM((parts, n_dev, 1, LANES), F32),
        pltpu.VMEM((2, n_dev // 2, q_count * OWN, LANES), BF16),
        pltpu.VMEM((n_dev, q_count * OWN, LANES), BF16),
        pltpu.VMEM((2, 1, LANES), F32),
        pltpu.VMEM((n_dev, 1, LANES), F32),
        pltpu.VMEM((2, rows, 2 * LANES), F32),
        pltpu.VMEM((rows * OWN, LANES), F32),
        pltpu.VMEM((rows * OWN, 2 * LANES), F32),
        pltpu.VMEM((rows, OWN * LANES), F32),
        pltpu.VMEM((rows, 2 * LANES), F32),
        pltpu.VMEM((tokens, chans), BF16),
        dma((len(operands),)), dma((2,)), dma, dma, dma((parts,)), dma((parts, 2)), dma((parts,)), dma((parts, 2)),
        dma, dma, dma, dma, dma,
    ]
    return pl.pallas_call(
        functools.partial(kernel, n_z),
        out_shape=jax.ShapeDtypeStruct((tokens, chans), BF16),
        in_specs=[pl.BlockSpec(memory_space=pl.ANY)] * len(operands),
        out_specs=pl.BlockSpec(memory_space=pl.ANY),
        scratch_shapes=scratch,
        compiler_params=pltpu.CompilerParams(collective_id=0, has_side_effects=True, vmem_limit_bytes=60 << 20),
    )(*operands)


def solution(mesh):
    placed = (
        P("ctx", "ch"),
        P("ctx", "ch"),
        P("ctx", "ch"),
        P(None, "ch"),
        P("ctx", "ch"),
        P("ch"),
    )
    n_z = mesh.shape["ctx"] // INNER
    return jax.shard_map(
        functools.partial(local, n_z), mesh=mesh, in_specs=placed, out_specs=P("ctx", "ch"), check_vma=False
    )
```

```python
import functools
import math

import jax
import jax.numpy as jnp
import numpy as np
from jax import lax
from jax.experimental import pallas as pl
from jax.experimental.pallas import tpu as pltpu
from jax.sharding import PartitionSpec as P

LANES = 128
OWN = 8
INNER = 4
F32 = jnp.float32
BF16 = jnp.bfloat16
MESH = pl.DeviceIdType.MESH
KNEE = 64.0
SPAN = 120.0
POWER = 2 * SPAN / math.log2(1 + KNEE)


def split_np(table):
    table = table.astype(np.float32)
    high = table.astype(BF16)
    low = (table - high.astype(np.float32)).astype(BF16)
    return high, low


def long_tables(rows):
    length = rows * LANES
    n1 = np.arange(rows)
    n2 = np.arange(LANES)
    first = np.pi * n1[None, :] * LANES / (2 * length) - 2 * np.pi * ((n1[:, None] * n1[None, :]) % rows) / rows
    twist = np.pi * n2[None, :] / (2 * length) - 2 * np.pi * ((n1[:, None] * n2[None, :]) % length) / length
    second = -2 * np.pi * ((n2[:, None] * n2[None, :]) % LANES) / LANES
    hi, lo = split_np(np.concatenate([np.cos(first), np.sin(first)], 0))
    col_fwd = np.concatenate([hi, hi, lo], 1)
    cos1, sin1 = np.cos(first).T, np.sin(first).T
    hi, lo = split_np(np.block([[cos1, sin1], [-sin1, cos1]]))
    col_inv = np.concatenate([hi, hi, lo], 1)
    cos2, sin2 = np.cos(second), np.sin(second)
    row = np.block([[cos2, sin2], [-sin2, cos2]])
    row_fwd = np.concatenate(split_np(row), 0)
    row_inv = np.concatenate(split_np(row.T), 0)
    turn = np.concatenate([np.cos(twist), np.sin(twist)], 0).astype(np.float32)
    return col_fwd, col_inv, row_fwd, row_inv, turn


def short_tables():
    size = 2 * LANES
    n = np.arange(size)
    k = np.arange(LANES)
    angle = 2 * np.pi * ((n[:, None] * k[None, :]) % size) / size
    re, im = np.cos(angle), -np.sin(angle)
    im[:, 0] = np.where(n % 2 == 0, 1.0, -1.0)
    fwd = np.concatenate(split_np(np.concatenate([re, im], 1)), 0)
    weight = np.where(k == 0, 1.0, 2.0) / size
    back = np.concatenate([(re * weight).T, (im * weight).T], 0)[:, LANES:]
    inv = np.concatenate(split_np(back), 1)
    return fwd, inv


def mm(a, b):
    return jnp.dot(a, b, preferred_element_type=F32)


def halves(x):
    high = x.astype(BF16)
    return high, (x - high.astype(F32)).astype(BF16)


def peak(x):
    top = jnp.max(jnp.max(jnp.abs(x), axis=0, keepdims=True), axis=1, keepdims=True)
    return jnp.broadcast_to(jnp.maximum(top, 1e-30), (1, LANES))


def encode(x, top):
    size = jnp.exp2(POWER * jnp.log2(1.0 + jnp.abs(x) * (KNEE / top)) - SPAN)
    return jnp.where(x < 0, -size, size)


def decode(code, top):
    size = (jnp.exp2((jnp.log2(jnp.abs(code)) + SPAN) * (1.0 / POWER)) - 1.0) * (top * (1.0 / KNEE))
    return jnp.where(code < 0, -size, size)


def along(block, table):
    high, low = halves(block)
    main = table[0 : 2 * LANES, :]
    return mm(high, main) + mm(low, main) + mm(high, table[2 * LANES :, :])


def kernel(
    n_z,
    og_any, ig_any, vi_any, sf_any, lf_any, skip_any, colf_any, coli_any, rowf_any, rowi_any, turn_any, shf_any, shi_any,
    out,
    og, ig, vi, sf, lf, skip, colf, coli, rowf, rowi, turn, shf, shi,
    halo, vt, igt, skipt, taps, keep, fsend, frecv, msend, mrecv, tsend, trecv, rsend, rrecv, usend, urecv,
    spec, xs, cross, carry, fin,
    in_sem, halo_sem, fs_sem, fr_sem, ms_sem, mr_sem, ts_sem, tr_sem, rs_sem, rr_sem, us_sem, ur_sem,
):
    n_dev = n_z * INNER
    half_z = n_z // 2
    half_dev = n_dev // 2
    order = [
        (vi_any, vi), (ig_any, ig), (shf_any, shf), (sf_any, sf), (lf_any, lf), (shi_any, shi), (og_any, og), (skip_any, skip),
        (colf_any, colf), (coli_any, coli), (rowf_any, rowf), (rowi_any, rowi), (turn_any, turn),
    ]
    loads = [pltpu.make_async_copy(src, dst, in_sem.at[i]) for i, (src, dst) in enumerate(order)]
    for copy in loads:
        copy.start()

    def wrap(x, n):
        return jnp.where(x >= n, x - n, x)

    me = lax.axis_index("ctx")
    my_z = me // INNER
    my_in = me - my_z * INNER
    my_x = my_in // 2
    my_core = my_in - my_x * 2
    partner = me + 1 - 2 * my_core
    my_half = jnp.where(my_z >= half_z, 1, 0)
    tokens, chans = vi.shape
    q_count = tokens // LANES
    rows = half_dev * q_count
    blocks = chans // LANES
    parts = q_count // 2
    per_block = LANES // OWN

    inners = [my_in] + [wrap(my_in + r, INNER) for r in range(1, INNER)]
    turns = []
    for d in range(1, n_z // 2):
        turns += [d, -d]
    turns += [n_z // 2, 0]
    ahead = {d: wrap(my_z + d + (n_z if d < 0 else 0), n_z) * INNER for d in turns}
    flip = {d: (-d if -d in ahead else d) for d in turns}
    planes = [jnp.where(my_core == 0, ahead[d], ahead[flip[d]]) for d in turns]
    peers = [z + i for z in planes for i in inners[1:] + inners[:1]][:-1]

    barrier = pltpu.get_barrier_semaphore()
    for p in peers[: n_dev - INNER][::-1] + peers[n_dev - INNER :]:
        pl.semaphore_signal(barrier, inc=1, device_id={"ctx": p}, device_id_type=MESH)

    def remote(src, dst, ssem, rsem, p):
        pltpu.make_async_remote_copy(
            src_ref=src, dst_ref=dst, send_sem=ssem, recv_sem=rsem, device_id={"ctx": p}, device_id_type=MESH
        ).start()

    def arrived(ref, sem):
        pltpu.make_async_copy(ref, ref, sem).wait()

    def send_all(src_of, dst, ssem, rsem):
        pltpu.make_async_copy(src_of(me), dst.at[me], rsem).start()
        for p in peers:
            remote(src_of(p), dst.at[me], ssem, rsem, p)

    def put_block(b, q):
        toks = slice(q * LANES, (q + 1) * LANES)
        lanes = slice(b * LANES, (b + 1) * LANES)
        vt[q + 1, lanes, :] = vi[toks, lanes].astype(F32).T.astype(BF16)
        igt[q, lanes, :] = ig[toks, lanes].astype(F32).T

    last_in = (my_z >= n_z - n_z // 4) & (my_x == 1)

    def enter():
        pl.semaphore_wait(barrier, n_dev - 1)

        @pl.when(me < n_dev - 1)
        def _():
            remote(vi_any.at[pl.ds(tokens - LANES, LANES), :], halo, halo_sem.at[0], halo_sem.at[1], me + 1)

    pl.when(last_in)(enter)
    loads[0].wait()
    loads[1].wait()
    for q in range(q_count):
        for b in range(blocks):
            put_block(b, q)

    loads[2].wait()
    loads[3].wait()
    lane = lax.broadcasted_iota(jnp.int32, (LANES, LANES), 1)
    for b in range(blocks):
        lanes = slice(b * LANES, (b + 1) * LANES)
        high, low = halves(sf[:, lanes].T)
        upper = shf[0:LANES, :]
        freq = mm(high, upper) + mm(low, upper) + mm(high, shf[2 * LANES : 3 * LANES, :])
        f_re, f_im = freq[:, 0:LANES], freq[:, LANES:]
        taps[0, lanes, :] = f_re
        taps[1, lanes, :] = jnp.where(lane == 0, 0.0, f_im)
        taps[2, lanes, :] = jnp.where(lane == 0, f_im, f_re)

    loads[4].wait()
    for g in range(n_dev // 2):
        for q in range(q_count):
            fsend[g, pl.ds(q, 1), :] = lf[pl.ds(g, 1), q * LANES : (q + 1) * LANES]
    loads[5].wait()

    def short(q):
        for b in range(blocks):
            lanes = slice(b * LANES, (b + 1) * LANES)
            window = jnp.concatenate([vt[q, lanes, :], vt[q + 1, lanes, :]], axis=1)
            freq = mm(window, shf[0 : 2 * LANES, :]) + mm(window, shf[2 * LANES :, :])
            re, im = freq[:, 0:LANES], freq[:, LANES:]
            f_re, f_zero, f_top = taps[0, lanes, :], taps[1, lanes, :], taps[2, lanes, :]
            prod = jnp.concatenate([re * f_re - im * f_zero, re * f_zero + im * f_top], axis=1)
            high, low = halves(prod)
            wide = mm(high, shi[...])
            keep[q, lanes, :] = igt[q, lanes, :] * (wide[:, 0:LANES] + wide[:, LANES:] + mm(low, shi[:, 0:LANES]))

    share = LANES // parts

    def pack(part):
        q = 2 * part
        top = peak(keep[q : q + 2].reshape(2 * chans, LANES))
        tsend[:, part * share : (part + 1) * share] = top[:, 0:share]
        first = encode(keep[q], top).reshape(n_dev, OWN, LANES)
        second = encode(keep[q + 1], top).reshape(n_dev, OWN, LANES)
        msend[part] = jnp.concatenate([first, second], axis=1).astype(BF16)

    for q in range(q_count - 1, 0, -1):
        short(q)
    for part in range(parts - 1, 0, -1):
        pack(part)

    pl.when(jnp.logical_not(last_in))(enter)

    def send_part(part):
        send_all(lambda p: msend.at[part, p], mrecv.at[part], ms_sem.at[part], mr_sem.at[part, my_half])

    my_pair = 2 * my_z + my_x
    for k in range(n_dev // 2):
        z, x = planes[k // 2], k % 2
        g = (z // 2) + wrap(my_x + 1 - x, 2)
        if k < n_dev // 2 - 1:
            remote(fsend.at[g], frecv.at[my_core, my_pair], fs_sem.at[0], fr_sem.at[0], 2 * g + my_core)
        else:
            pltpu.make_async_copy(fsend.at[my_pair], frecv.at[my_core, my_pair], fr_sem.at[0]).start()
    for part in range(parts - 1, 0, -1):
        send_part(part)

    @pl.when(me > 0)
    def _():
        pltpu.make_async_copy(halo, halo, halo_sem.at[1]).wait()

    for b in range(blocks):
        lanes = slice(b * LANES, (b + 1) * LANES)
        before = halo[:, lanes].astype(F32).T
        vt[0, lanes, :] = jnp.where(me > 0, before, 0.0).astype(BF16)
    short(0)
    pack(0)
    send_part(0)
    send_all(lambda p: tsend, trecv, ts_sem, tr_sem.at[my_half])
    arrived(frecv.at[my_core], fr_sem.at[0])
    remote(frecv.at[my_core], frecv.at[my_core], fs_sem.at[1], fr_sem.at[1], partner)

    for i in range(6, len(order)):
        loads[i].wait()
    for b in range(blocks):
        lanes = slice(b * LANES, (b + 1) * LANES)
        skipt[lanes, :] = jnp.broadcast_to(skip[:, lanes], (LANES, LANES)).T

    turn_re = turn[0:rows, :]
    turn_im = turn[rows:, :]

    def forward(block):
        high, low = halves(block)
        first = mm(colf[...], jnp.concatenate([high, low, high], axis=0))
        pieces = []
        for k in range(block.shape[1] // LANES):
            re = first[0:rows, k * LANES : (k + 1) * LANES]
            im = first[rows:, k * LANES : (k + 1) * LANES]
            pieces.append(jnp.concatenate([re * turn_re - im * turn_im, re * turn_im + im * turn_re], axis=1))
        return along(jnp.concatenate(pieces, axis=0), rowf[...])

    def backward(block, keep_rows):
        mid = along(block, rowi[...])
        reals, imags = [], []
        for c in range(OWN):
            re = mid[c * rows : (c + 1) * rows, 0:LANES]
            im = mid[c * rows : (c + 1) * rows, LANES:]
            reals.append(re * turn_re + im * turn_im)
            imags.append(im * turn_re - re * turn_im)
        high, low = halves(jnp.concatenate([jnp.concatenate(reals, axis=1), jnp.concatenate(imags, axis=1)], axis=0))
        return mm(coli[0:keep_rows, :], jnp.concatenate([high, low, high], axis=0))

    def times(spectra, which):
        h_re = spec[which, :, 0:LANES]
        h_im = spec[which, :, LANES:]
        out = []
        for c in range(OWN):
            re = spectra[c * rows : (c + 1) * rows, 0:LANES]
            im = spectra[c * rows : (c + 1) * rows, LANES:]
            out.append(jnp.concatenate([re * h_re - im * h_im, re * h_im + im * h_re], axis=1))
        return jnp.concatenate(out, axis=0)

    arrived(frecv.at[0], fr_sem.at[1])
    for s in range(n_dev):
        which, at = s // half_dev, s % half_dev
        fin[q_count * at : q_count * (at + 1), which * LANES : (which + 1) * LANES] = frecv[s % 2, s // 2]
    both = forward(fin[...]) * (1.0 / (rows * LANES))
    spec[0] = both[0:rows]
    spec[1] = both[rows:]

    def owned(half):
        span = pl.ds(half * half_dev, half_dev)
        got = []
        for part in range(parts):
            arrived(mrecv.at[part, span], mr_sem.at[part, half])
        arrived(trecv.at[span], tr_sem.at[half])
        tops = trecv[span].reshape(half_dev, LANES)
        for part in range(parts):
            one = tops
            if parts > 1:
                at = lax.broadcasted_iota(jnp.int32, (half_dev, LANES), 1) // share
                one = jnp.zeros_like(tops)
                for k in range(parts):
                    moved = pltpu.roll(tops, (k - part) * share % LANES, 1) if k != part else tops
                    one = jnp.where(at == k, moved, one)
            got.append(decode(mrecv[part, span].astype(F32), one.reshape(half_dev, 1, LANES)))
        xs[...] = jnp.concatenate(got, axis=1).reshape(rows * OWN, LANES)
        return jnp.concatenate([xs[pl.ds(c, rows, stride=OWN), :] for c in range(OWN)], axis=1)

    def give_back(half, result):
        top = peak(result)
        usend[half] = top
        wide = jnp.concatenate([top] * OWN, axis=1)
        code = encode(result, wide)
        for c in range(OWN):
            xs[pl.ds(c, rows, stride=OWN), :] = code[:, c * LANES : (c + 1) * LANES]
        rsend[half] = xs[...].reshape(half_dev, q_count * OWN, LANES).astype(BF16)
        for k in range(half_z):
            z = wrap(wrap(my_z, half_z) + k, half_z) if k else wrap(my_z, half_z)
            for r in range(INNER):
                at = z * INNER + inners[r]
                p = half * half_dev + at

                def away():
                    remote(rsend.at[half, at], rrecv.at[me], rs_sem, rr_sem, p)
                    remote(usend.at[half], urecv.at[me], us_sem, ur_sem, p)

                if k or r:
                    away()
                else:
                    pl.when(my_half != half)(away)

                    @pl.when(my_half == half)
                    def _():
                        pltpu.make_async_copy(rsend.at[half, at], rrecv.at[me], rr_sem).start()
                        pltpu.make_async_copy(usend.at[half], urecv.at[me], ur_sem).start()

    spectra = forward(owned(0))
    result = backward(times(spectra, 0), 2 * rows)
    carry[...] = result[rows:]
    give_back(0, result[0:rows])
    cross[...] = times(spectra, 1)
    spectra = forward(owned(1))
    give_back(1, backward(times(spectra, 0) + cross[...], rows) + carry[...])

    arrived(rrecv, rr_sem)
    arrived(urecv, ur_sem)
    for q in range(q_count):
        toks = slice(q * LANES, (q + 1) * LANES)
        code = rrecv[:, (q // 2) * 2 * OWN : (q // 2 + 1) * 2 * OWN, :].astype(F32)[:, (q % 2) * OWN : (q % 2 + 1) * OWN, :]
        total = decode(code, urecv[...]).reshape(chans, LANES) + skipt[...] * keep[q]
        for b in range(blocks):
            lanes = slice(b * LANES, (b + 1) * LANES)
            out[toks, lanes] = (og[toks, lanes].astype(F32) * total[lanes, :].T).astype(BF16)

    sent = pl.ds(0, n_dev - 1)

    @pl.when(me < n_dev - 1)
    def _():
        arrived(halo, halo_sem.at[0])

    arrived(frecv.at[0, pl.ds(0, n_dev // 2 - 1)], fs_sem.at[0])
    arrived(frecv.at[0], fs_sem.at[1])
    for part in range(parts):
        arrived(mrecv.at[part, sent], ms_sem.at[part])
    arrived(trecv.at[sent], ts_sem)
    arrived(rrecv.at[sent], rs_sem)
    arrived(urecv.at[sent], us_sem)


def local(n_z, output_gate, input_gate, value_input, short_filter, long_filter, skip_gain):
    n_dev = n_z * INNER
    tokens, chans = value_input.shape
    q_count = tokens // LANES
    parts = q_count // 2
    rows = n_dev * q_count // 2
    tabs = [jnp.asarray(t) for t in long_tables(rows) + short_tables()]
    operands = [output_gate, input_gate, value_input, short_filter, long_filter.T, skip_gain.reshape(1, chans)] + tabs
    dma = pltpu.SemaphoreType.DMA
    scratch = [pltpu.VMEM(x.shape, x.dtype) for x in operands]
    scratch += [
        pltpu.VMEM((LANES, chans), BF16),
        pltpu.VMEM((q_count + 1, chans, LANES), BF16),
        pltpu.VMEM((q_count, chans, LANES), F32),
        pltpu.VMEM((chans, LANES), F32),
        pltpu.VMEM((3, chans, LANES), F32),
        pltpu.VMEM((q_count, chans, LANES), F32),
        pltpu.VMEM((n_dev // 2, q_count, LANES), F32),
        pltpu.VMEM((2, n_dev // 2, q_count, LANES), F32),
        pltpu.VMEM((parts, n_dev, 2 * OWN, LANES), BF16),
        pltpu.VMEM((parts, n_dev, 2 * OWN, LANES), BF16),
        pltpu.VMEM((1, LANES), F32),
        pltpu.VMEM((n_dev, 1, LANES), F32),
        pltpu.VMEM((2, n_dev // 2, q_count * OWN, LANES), BF16),
        pltpu.VMEM((n_dev, q_count * OWN, LANES), BF16),
        pltpu.VMEM((2, 1, LANES), F32),
        pltpu.VMEM((n_dev, 1, LANES), F32),
        pltpu.VMEM((2, rows, 2 * LANES), F32),
        pltpu.VMEM((rows * OWN, LANES), F32),
        pltpu.VMEM((rows * OWN, 2 * LANES), F32),
        pltpu.VMEM((rows, OWN * LANES), F32),
        pltpu.VMEM((rows, 2 * LANES), F32),
        dma((len(operands),)), dma((2,)), dma((2,)), dma((2,)), dma((parts,)), dma((parts, 2)), dma, dma((2,)),
        dma, dma, dma, dma,
    ]
    return pl.pallas_call(
        functools.partial(kernel, n_z),
        out_shape=pltpu.VMEM((tokens, chans), BF16),
        in_specs=[pl.BlockSpec(memory_space=pl.ANY)] * len(operands),
        out_specs=pl.BlockSpec(memory_space=pltpu.VMEM),
        scratch_shapes=scratch,
        compiler_params=pltpu.CompilerParams(collective_id=0, has_side_effects=True, vmem_limit_bytes=60 << 20),
    )(*operands)


def solution(mesh):
    placed = (
        P("ctx", "ch"),
        P("ctx", "ch"),
        P("ctx", "ch"),
        P(None, "ch"),
        P("ctx", "ch"),
        P("ch"),
    )
    n_z = mesh.shape["ctx"] // INNER
    return jax.shard_map(
        functools.partial(local, n_z), mesh=mesh, in_specs=placed, out_specs=P("ctx", "ch"), check_vma=False
    )
```

```python
import functools
import math

import jax
import jax.numpy as jnp
import numpy as np
from jax import lax
from jax.experimental import pallas as pl
from jax.experimental.pallas import tpu as pltpu
from jax.sharding import PartitionSpec as P

LANES = 128
OWN = 8
INNER = 4
F32 = jnp.float32
BF16 = jnp.bfloat16
MESH = pl.DeviceIdType.MESH
KNEE = 64.0
SPAN = 120.0
POWER = 2 * SPAN / math.log2(1 + KNEE)


def split_np(table):
    table = table.astype(np.float32)
    high = table.astype(BF16)
    low = (table - high.astype(np.float32)).astype(BF16)
    return high, low


def long_tables(rows):
    length = rows * LANES
    n1 = np.arange(rows)
    n2 = np.arange(LANES)
    first = np.pi * n1[None, :] * LANES / (2 * length) - 2 * np.pi * ((n1[:, None] * n1[None, :]) % rows) / rows
    twist = np.pi * n2[None, :] / (2 * length) - 2 * np.pi * ((n1[:, None] * n2[None, :]) % length) / length
    second = -2 * np.pi * ((n2[:, None] * n2[None, :]) % LANES) / LANES
    hi, lo = split_np(np.concatenate([np.cos(first), np.sin(first)], 0))
    col_fwd = np.concatenate([hi, hi, lo], 1)
    cos1, sin1 = np.cos(first).T, np.sin(first).T
    hi, lo = split_np(np.block([[cos1, sin1], [-sin1, cos1]]))
    col_inv = np.concatenate([hi, hi, lo], 1)
    cos2, sin2 = np.cos(second), np.sin(second)
    row = np.block([[cos2, sin2], [-sin2, cos2]])
    row_fwd = np.concatenate(split_np(row), 0)
    row_inv = np.concatenate(split_np(row.T), 0)
    turn = np.concatenate([np.cos(twist), np.sin(twist)], 0).astype(np.float32)
    return col_fwd, col_inv, row_fwd, row_inv, turn


def short_tables():
    size = 2 * LANES
    n = np.arange(size)
    k = np.arange(LANES)
    angle = 2 * np.pi * ((n[:, None] * k[None, :]) % size) / size
    re, im = np.cos(angle), -np.sin(angle)
    im[:, 0] = np.where(n % 2 == 0, 1.0, -1.0)
    fwd = np.concatenate(split_np(np.concatenate([re, im], 1)), 0)
    weight = np.where(k == 0, 1.0, 2.0) / size
    back = np.concatenate([(re * weight).T, (im * weight).T], 0)[:, LANES:]
    inv = np.concatenate(split_np(back), 1)
    return fwd, inv


def mm(a, b):
    return jnp.dot(a, b, preferred_element_type=F32)


def halves(x):
    high = x.astype(BF16)
    return high, (x - high.astype(F32)).astype(BF16)


def peak(x):
    top = jnp.max(jnp.max(jnp.abs(x), axis=0, keepdims=True), axis=1, keepdims=True)
    return jnp.broadcast_to(jnp.maximum(top, 1e-30), (1, LANES))


def encode(x, top):
    size = jnp.exp2(POWER * jnp.log2(1.0 + jnp.abs(x) * (KNEE / top)) - SPAN)
    return jnp.where(x < 0, -size, size)


def decode(code, top):
    size = (jnp.exp2((jnp.log2(jnp.abs(code)) + SPAN) * (1.0 / POWER)) - 1.0) * (top * (1.0 / KNEE))
    return jnp.where(code < 0, -size, size)


def along(block, table):
    high, low = halves(block)
    main = table[0 : 2 * LANES, :]
    return mm(high, main) + mm(low, main) + mm(high, table[2 * LANES :, :])


def kernel(
    n_z,
    og_any, ig_any, vi_any, sf_any, lf_any, skip_any, colf_any, coli_any, rowf_any, rowi_any, turn_any, shf_any, shi_any,
    out,
    og, ig, vi, sf, lf, skip, colf, coli, rowf, rowi, turn, shf, shi,
    halo, vt, igt, skipt, taps, keep, fsend, frecv, msend, mrecv, tsend, trecv, rsend, rrecv, usend, urecv,
    spec, xs, cross, carry, ready, fin,
    in_sem, halo_sem, fs_sem, fr_sem, ms_sem, mr_sem, ts_sem, tr_sem, rs_sem, rr_sem, us_sem, ur_sem,
):
    n_dev = n_z * INNER
    half_z = n_z // 2
    half_dev = n_dev // 2
    order = [
        (vi_any, vi), (ig_any, ig), (shf_any, shf), (sf_any, sf), (lf_any, lf), (shi_any, shi), (og_any, og), (skip_any, skip),
        (colf_any, colf), (coli_any, coli), (rowf_any, rowf), (rowi_any, rowi), (turn_any, turn),
    ]
    loads = [pltpu.make_async_copy(src, dst, in_sem.at[i]) for i, (src, dst) in enumerate(order)]
    for copy in loads:
        copy.start()

    def wrap(x, n):
        return jnp.where(x >= n, x - n, x)

    me = lax.axis_index("ctx")
    my_z = me // INNER
    my_in = me - my_z * INNER
    my_x = my_in // 2
    my_core = my_in - my_x * 2
    partner = me + 1 - 2 * my_core
    my_half = jnp.where(my_z >= half_z, 1, 0)
    tokens, chans = vi.shape
    q_count = tokens // LANES
    rows = half_dev * q_count
    blocks = chans // LANES
    parts = q_count // 2
    per_block = LANES // OWN

    inners = [my_in] + [wrap(my_in + r, INNER) for r in range(1, INNER)]
    turns = [n_z // 2]
    for d in range(n_z // 2 - 1, 0, -1):
        turns += [d, -d]
    turns += [0]
    ahead = {d: wrap(my_z + d + (n_z if d < 0 else 0), n_z) * INNER for d in turns}
    flip = {d: (-d if -d in ahead else d) for d in turns}
    planes = [jnp.where(my_core == 0, ahead[d], ahead[flip[d]]) for d in turns]
    peers = [z + i for z in planes for i in inners[1:] + inners[:1]][:-1]

    barrier = pltpu.get_barrier_semaphore()
    for p in peers:
        pl.semaphore_signal(barrier, inc=1, device_id={"ctx": p}, device_id_type=MESH)

    def remote(src, dst, ssem, rsem, p):
        pltpu.make_async_remote_copy(
            src_ref=src, dst_ref=dst, send_sem=ssem, recv_sem=rsem, device_id={"ctx": p}, device_id_type=MESH
        ).start()

    def arrived(ref, sem):
        pltpu.make_async_copy(ref, ref, sem).wait()

    def send_all(src_of, dst, ssem, rsem):
        pltpu.make_async_copy(src_of(me), dst.at[me], rsem).start()
        for p in peers:
            remote(src_of(p), dst.at[me], ssem, rsem, p)

    def put_block(b, q):
        toks = slice(q * LANES, (q + 1) * LANES)
        lanes = slice(b * LANES, (b + 1) * LANES)
        vt[q + 1, lanes, :] = vi[toks, lanes].astype(F32).T.astype(BF16)
        igt[q, lanes, :] = ig[toks, lanes].astype(F32).T

    last_in = (my_z >= n_z - n_z // 4) & (my_x == 1)

    def enter():
        pl.semaphore_wait(barrier, n_dev - 1)

        @pl.when(me < n_dev - 1)
        def _():
            remote(vi_any.at[pl.ds(tokens - LANES, LANES), :], halo, halo_sem.at[0], halo_sem.at[1], me + 1)

    pl.when(last_in)(enter)
    loads[0].wait()
    loads[1].wait()
    for q in range(q_count):
        for b in range(blocks):
            put_block(b, q)

    loads[2].wait()
    loads[3].wait()
    lane = lax.broadcasted_iota(jnp.int32, (LANES, LANES), 1)
    for b in range(blocks):
        lanes = slice(b * LANES, (b + 1) * LANES)
        high, low = halves(sf[:, lanes].T)
        upper = shf[0:LANES, :]
        freq = mm(high, upper) + mm(low, upper) + mm(high, shf[2 * LANES : 3 * LANES, :])
        f_re, f_im = freq[:, 0:LANES], freq[:, LANES:]
        taps[0, lanes, :] = f_re
        taps[1, lanes, :] = jnp.where(lane == 0, 0.0, f_im)
        taps[2, lanes, :] = jnp.where(lane == 0, f_im, f_re)

    loads[4].wait()
    for g in range(n_dev // 2):
        for q in range(q_count):
            fsend[g, pl.ds(q, 1), :] = lf[pl.ds(g, 1), q * LANES : (q + 1) * LANES]
    loads[5].wait()

    def short(q):
        for b in range(blocks):
            lanes = slice(b * LANES, (b + 1) * LANES)
            window = jnp.concatenate([vt[q, lanes, :], vt[q + 1, lanes, :]], axis=1)
            freq = mm(window, shf[0 : 2 * LANES, :]) + mm(window, shf[2 * LANES :, :])
            re, im = freq[:, 0:LANES], freq[:, LANES:]
            f_re, f_zero, f_top = taps[0, lanes, :], taps[1, lanes, :], taps[2, lanes, :]
            prod = jnp.concatenate([re * f_re - im * f_zero, re * f_zero + im * f_top], axis=1)
            high, low = halves(prod)
            wide = mm(high, shi[...])
            keep[q, lanes, :] = igt[q, lanes, :] * (wide[:, 0:LANES] + wide[:, LANES:] + mm(low, shi[:, 0:LANES]))

    share = LANES // parts

    def pack(part):
        q = 2 * part
        top = peak(keep[q : q + 2].reshape(2 * chans, LANES))
        tsend[:, part * share : (part + 1) * share] = top[:, 0:share]
        first = encode(keep[q], top).reshape(n_dev, OWN, LANES)
        second = encode(keep[q + 1], top).reshape(n_dev, OWN, LANES)
        msend[part] = jnp.concatenate([first, second], axis=1).astype(BF16)

    for q in range(q_count - 1, 0, -1):
        short(q)
    for part in range(parts - 1, 0, -1):
        pack(part)

    pl.when(jnp.logical_not(last_in))(enter)

    def send_part(part):
        send_all(lambda p: msend.at[part, p], mrecv.at[part], ms_sem.at[part], mr_sem.at[part, my_half])

    my_pair = 2 * my_z + my_x
    for k in range(n_dev // 2):
        z, x = planes[k // 2], k % 2
        g = (z // 2) + wrap(my_x + 1 - x, 2)
        if k < n_dev // 2 - 1:
            remote(fsend.at[g], frecv.at[my_core, my_pair], fs_sem.at[0], fr_sem.at[0], 2 * g + my_core)
        else:
            pltpu.make_async_copy(fsend.at[my_pair], frecv.at[my_core, my_pair], fr_sem.at[0]).start()
    for part in range(parts - 1, 0, -1):
        send_part(part)

    @pl.when(me > 0)
    def _():
        pltpu.make_async_copy(halo, halo, halo_sem.at[1]).wait()

    for b in range(blocks):
        lanes = slice(b * LANES, (b + 1) * LANES)
        before = halo[:, lanes].astype(F32).T
        vt[0, lanes, :] = jnp.where(me > 0, before, 0.0).astype(BF16)
    short(0)
    pack(0)
    send_all(lambda p: tsend, trecv, ts_sem, tr_sem.at[my_half])
    send_part(0)
    arrived(frecv.at[my_core], fr_sem.at[0])
    remote(frecv.at[my_core], frecv.at[my_core], fs_sem.at[1], fr_sem.at[1], partner)

    for i in range(6, len(order)):
        loads[i].wait()
    for b in range(blocks):
        lanes = slice(b * LANES, (b + 1) * LANES)
        skipt[lanes, :] = jnp.broadcast_to(skip[:, lanes], (LANES, LANES)).T

    turn_re = turn[0:rows, :]
    turn_im = turn[rows:, :]

    def forward(block):
        high, low = halves(block)
        first = mm(colf[...], jnp.concatenate([high, low, high], axis=0))
        pieces = []
        for k in range(block.shape[1] // LANES):
            re = first[0:rows, k * LANES : (k + 1) * LANES]
            im = first[rows:, k * LANES : (k + 1) * LANES]
            pieces.append(jnp.concatenate([re * turn_re - im * turn_im, re * turn_im + im * turn_re], axis=1))
        return along(jnp.concatenate(pieces, axis=0), rowf[...])

    def backward(block):
        mid = along(block, rowi[...])
        reals, imags = [], []
        for c in range(OWN):
            re = mid[c * rows : (c + 1) * rows, 0:LANES]
            im = mid[c * rows : (c + 1) * rows, LANES:]
            reals.append(re * turn_re + im * turn_im)
            imags.append(im * turn_re - re * turn_im)
        high, low = halves(jnp.concatenate([jnp.concatenate(reals, axis=1), jnp.concatenate(imags, axis=1)], axis=0))
        return jnp.concatenate([high, low, high], axis=0)

    def times(spectra, which):
        h_re = spec[which, :, 0:LANES]
        h_im = spec[which, :, LANES:]
        out = []
        for c in range(OWN):
            re = spectra[c * rows : (c + 1) * rows, 0:LANES]
            im = spectra[c * rows : (c + 1) * rows, LANES:]
            out.append(jnp.concatenate([re * h_re - im * h_im, re * h_im + im * h_re], axis=1))
        return jnp.concatenate(out, axis=0)

    arrived(frecv.at[0], fr_sem.at[1])
    for s in range(n_dev):
        which, at = s // half_dev, s % half_dev
        fin[q_count * at : q_count * (at + 1), which * LANES : (which + 1) * LANES] = frecv[s % 2, s // 2]
    both = forward(fin[...]) * (1.0 / (rows * LANES))
    spec[0] = both[0:rows]
    spec[1] = both[rows:]

    def owned(half):
        span = pl.ds(half * half_dev, half_dev)
        got = []
        for part in range(parts):
            arrived(mrecv.at[part, span], mr_sem.at[part, half])
        arrived(trecv.at[span], tr_sem.at[half])
        tops = trecv[span].reshape(half_dev, LANES)
        for part in range(parts):
            one = tops
            if parts > 1:
                at = lax.broadcasted_iota(jnp.int32, (half_dev, LANES), 1) // share
                one = jnp.zeros_like(tops)
                for k in range(parts):
                    moved = pltpu.roll(tops, (k - part) * share % LANES, 1) if k != part else tops
                    one = jnp.where(at == k, moved, one)
            got.append(decode(mrecv[part, span].astype(F32), one.reshape(half_dev, 1, LANES)))
        xs[...] = jnp.concatenate(got, axis=1).reshape(rows * OWN, LANES)
        return jnp.concatenate([xs[pl.ds(c, rows, stride=OWN), :] for c in range(OWN)], axis=1)

    def give_back(half, result):
        top = peak(result)
        usend[half] = top
        wide = jnp.concatenate([top] * OWN, axis=1)
        code = encode(result, wide)
        for c in range(OWN):
            xs[pl.ds(c, rows, stride=OWN), :] = code[:, c * LANES : (c + 1) * LANES]
        rsend[half] = xs[...].reshape(half_dev, q_count * OWN, LANES).astype(BF16)
        for z in range(half_z):
            for i in inners[1:] + inners[:1]:
                at = z * INNER + i
                p = half * half_dev + at

                def away():
                    remote(rsend.at[half, at], rrecv.at[me], rs_sem, rr_sem, p)
                    remote(usend.at[half], urecv.at[me], us_sem, ur_sem, p)

                if i is not inners[0]:
                    away()
                    continue
                pl.when(my_z != half * half_z + z)(away)

                @pl.when(my_z == half * half_z + z)
                def _():
                    pltpu.make_async_copy(rsend.at[half, at], rrecv.at[me], rr_sem).start()
                    pltpu.make_async_copy(usend.at[half], urecv.at[me], ur_sem).start()

    spectra = forward(owned(0))
    ready[...] = backward(times(spectra, 0))
    give_back(0, mm(coli[0:rows, :], ready[...]))
    carry[...] = mm(coli[rows:, :], ready[...])
    cross[...] = times(spectra, 1)
    spectra = forward(owned(1))
    give_back(1, mm(coli[0:rows, :], backward(times(spectra, 0) + cross[...])) + carry[...])

    arrived(rrecv, rr_sem)
    arrived(urecv, ur_sem)
    for q in range(q_count):
        toks = slice(q * LANES, (q + 1) * LANES)
        code = rrecv[:, (q // 2) * 2 * OWN : (q // 2 + 1) * 2 * OWN, :].astype(F32)[:, (q % 2) * OWN : (q % 2 + 1) * OWN, :]
        total = decode(code, urecv[...]).reshape(chans, LANES) + skipt[...] * keep[q]
        for b in range(blocks):
            lanes = slice(b * LANES, (b + 1) * LANES)
            out[toks, lanes] = (og[toks, lanes].astype(F32) * total[lanes, :].T).astype(BF16)

    sent = pl.ds(0, n_dev - 1)

    @pl.when(me < n_dev - 1)
    def _():
        arrived(halo, halo_sem.at[0])

    arrived(frecv.at[0, pl.ds(0, n_dev // 2 - 1)], fs_sem.at[0])
    arrived(frecv.at[0], fs_sem.at[1])
    for part in range(parts):
        arrived(mrecv.at[part, sent], ms_sem.at[part])
    arrived(trecv.at[sent], ts_sem)
    arrived(rrecv.at[sent], rs_sem)
    arrived(urecv.at[sent], us_sem)


def local(n_z, output_gate, input_gate, value_input, short_filter, long_filter, skip_gain):
    n_dev = n_z * INNER
    tokens, chans = value_input.shape
    q_count = tokens // LANES
    parts = q_count // 2
    rows = n_dev * q_count // 2
    tabs = [jnp.asarray(t) for t in long_tables(rows) + short_tables()]
    operands = [output_gate, input_gate, value_input, short_filter, long_filter.T, skip_gain.reshape(1, chans)] + tabs
    dma = pltpu.SemaphoreType.DMA
    scratch = [pltpu.VMEM(x.shape, x.dtype) for x in operands]
    scratch += [
        pltpu.VMEM((LANES, chans), BF16),
        pltpu.VMEM((q_count + 1, chans, LANES), BF16),
        pltpu.VMEM((q_count, chans, LANES), F32),
        pltpu.VMEM((chans, LANES), F32),
        pltpu.VMEM((3, chans, LANES), F32),
        pltpu.VMEM((q_count, chans, LANES), F32),
        pltpu.VMEM((n_dev // 2, q_count, LANES), F32),
        pltpu.VMEM((2, n_dev // 2, q_count, LANES), F32),
        pltpu.VMEM((parts, n_dev, 2 * OWN, LANES), BF16),
        pltpu.VMEM((parts, n_dev, 2 * OWN, LANES), BF16),
        pltpu.VMEM((1, LANES), F32),
        pltpu.VMEM((n_dev, 1, LANES), F32),
        pltpu.VMEM((2, n_dev // 2, q_count * OWN, LANES), BF16),
        pltpu.VMEM((n_dev, q_count * OWN, LANES), BF16),
        pltpu.VMEM((2, 1, LANES), F32),
        pltpu.VMEM((n_dev, 1, LANES), F32),
        pltpu.VMEM((2, rows, 2 * LANES), F32),
        pltpu.VMEM((rows * OWN, LANES), F32),
        pltpu.VMEM((rows * OWN, 2 * LANES), F32),
        pltpu.VMEM((rows, OWN * LANES), F32),
        pltpu.VMEM((6 * rows, OWN * LANES), BF16),
        pltpu.VMEM((rows, 2 * LANES), F32),
        dma((len(operands),)), dma((2,)), dma((2,)), dma((2,)), dma((parts,)), dma((parts, 2)), dma, dma((2,)),
        dma, dma, dma, dma,
    ]
    return pl.pallas_call(
        functools.partial(kernel, n_z),
        out_shape=pltpu.VMEM((tokens, chans), BF16),
        in_specs=[pl.BlockSpec(memory_space=pl.ANY)] * len(operands),
        out_specs=pl.BlockSpec(memory_space=pltpu.VMEM),
        scratch_shapes=scratch,
        compiler_params=pltpu.CompilerParams(collective_id=0, has_side_effects=True, vmem_limit_bytes=60 << 20),
    )(*operands)


def solution(mesh):
    placed = (
        P("ctx", "ch"),
        P("ctx", "ch"),
        P("ctx", "ch"),
        P(None, "ch"),
        P("ctx", "ch"),
        P("ch"),
    )
    n_z = mesh.shape["ctx"] // INNER
    return jax.shard_map(
        functools.partial(local, n_z), mesh=mesh, in_specs=placed, out_specs=P("ctx", "ch"), check_vma=False
    )
```

```python
import functools
import math

import jax
import jax.numpy as jnp
import numpy as np
from jax import lax
from jax.experimental import pallas as pl
from jax.experimental.pallas import tpu as pltpu
from jax.sharding import PartitionSpec as P

LANES = 128
OWN = 8
INNER = 4
F32 = jnp.float32
BF16 = jnp.bfloat16
MESH = pl.DeviceIdType.MESH
KNEE = 64.0
SPAN = 120.0
POWER = 2 * SPAN / math.log2(1 + KNEE)


def split_np(table):
    table = table.astype(np.float32)
    high = table.astype(BF16)
    low = (table - high.astype(np.float32)).astype(BF16)
    return high, low


def long_tables(rows):
    length = rows * LANES
    n1 = np.arange(rows)
    n2 = np.arange(LANES)
    first = np.pi * n1[None, :] * LANES / (2 * length) - 2 * np.pi * ((n1[:, None] * n1[None, :]) % rows) / rows
    twist = np.pi * n2[None, :] / (2 * length) - 2 * np.pi * ((n1[:, None] * n2[None, :]) % length) / length
    second = -2 * np.pi * ((n2[:, None] * n2[None, :]) % LANES) / LANES
    hi, lo = split_np(np.concatenate([np.cos(first), np.sin(first)], 0))
    col_fwd = np.concatenate([hi, hi, lo], 1)
    cos1, sin1 = np.cos(first).T, np.sin(first).T
    hi, lo = split_np(np.block([[cos1, sin1], [-sin1, cos1]]))
    col_inv = np.concatenate([hi, hi, lo], 1)
    cos2, sin2 = np.cos(second), np.sin(second)
    row = np.block([[cos2, sin2], [-sin2, cos2]])
    hi, lo = split_np(row)
    row_fwd = np.concatenate([hi, hi, lo], 0)
    hi, lo = split_np(row.T)
    row_inv = np.concatenate([hi, hi, lo], 0)
    turn = np.concatenate([np.cos(twist), np.sin(twist)], 0).astype(np.float32)
    return col_fwd, col_inv, row_fwd, row_inv, turn


def short_tables():
    size = 2 * LANES
    n = np.arange(size)
    k = np.arange(LANES)
    angle = 2 * np.pi * ((n[:, None] * k[None, :]) % size) / size
    re, im = np.cos(angle), -np.sin(angle)
    im[:, 0] = np.where(n % 2 == 0, 1.0, -1.0)
    fwd = np.concatenate(split_np(np.concatenate([re, im], 1)), 0)
    weight = np.where(k == 0, 1.0, 2.0) / size
    back = np.concatenate([(re * weight).T, (im * weight).T], 0)[:, LANES:]
    inv = np.concatenate(split_np(back), 1)
    return fwd, inv


def mm(a, b):
    return jnp.dot(a, b, preferred_element_type=F32)


def halves(x):
    high = x.astype(BF16)
    return high, (x - high.astype(F32)).astype(BF16)


def peak(x):
    top = jnp.max(jnp.max(jnp.abs(x), axis=0, keepdims=True), axis=1, keepdims=True)
    return jnp.broadcast_to(jnp.maximum(top, 1e-30), (1, LANES))


def encode(x, top):
    size = jnp.exp2(POWER * jnp.log2(1.0 + jnp.abs(x) * (KNEE / top)) - SPAN)
    return jnp.where(x < 0, -size, size)


def decode(code, top):
    size = (jnp.exp2((jnp.log2(jnp.abs(code)) + SPAN) * (1.0 / POWER)) - 1.0) * (top * (1.0 / KNEE))
    return jnp.where(code < 0, -size, size)


def along(block, table):
    high, low = halves(block)
    return mm(jnp.concatenate([high, low, high], axis=1), table)


def kernel(
    n_z,
    og_any, ig_any, vi_any, sf_any, lf_any, skip_any, colf_any, coli_any, rowf_any, rowi_any, turn_any, shf_any, shi_any,
    out,
    og, ig, vi, sf, lf, skip, colf, coli, rowf, rowi, turn, shf, shi,
    halo, vt, igt, skipt, taps, keep, fsend, frecv, msend, mrecv, tsend, trecv, rsend, rrecv, usend, urecv,
    spec, xs, cross, carry, ready, fin,
    in_sem, halo_sem, fs_sem, fr_sem, ms_sem, mr_sem, ts_sem, tr_sem, rs_sem, rr_sem, us_sem, ur_sem,
):
    n_dev = n_z * INNER
    half_z = n_z // 2
    half_dev = n_dev // 2
    order = [
        (vi_any, vi), (ig_any, ig), (shf_any, shf), (sf_any, sf), (lf_any, lf), (shi_any, shi), (og_any, og), (skip_any, skip),
        (colf_any, colf), (coli_any, coli), (rowf_any, rowf), (rowi_any, rowi), (turn_any, turn),
    ]
    loads = [pltpu.make_async_copy(src, dst, in_sem.at[i]) for i, (src, dst) in enumerate(order)]
    for copy in loads:
        copy.start()

    def wrap(x, n):
        return jnp.where(x >= n, x - n, x)

    me = lax.axis_index("ctx")
    my_z = me // INNER
    my_in = me - my_z * INNER
    my_x = my_in // 2
    my_core = my_in - my_x * 2
    partner = me + 1 - 2 * my_core
    my_half = jnp.where(my_z >= half_z, 1, 0)
    tokens, chans = vi.shape
    q_count = tokens // LANES
    rows = half_dev * q_count
    blocks = chans // LANES
    parts = q_count // 2
    per_block = LANES // OWN

    inners = [my_in] + [wrap(my_in + r, INNER) for r in range(1, INNER)]
    turns = [n_z // 2]
    for d in range(n_z // 2 - 1, 0, -1):
        turns += [d, -d]
    turns += [0]
    ahead = {d: wrap(my_z + d + (n_z if d < 0 else 0), n_z) * INNER for d in turns}
    flip = {d: (-d if -d in ahead else d) for d in turns}
    planes = [jnp.where(my_core == 0, ahead[d], ahead[flip[d]]) for d in turns]
    peers = [z + i for z in planes for i in inners[1:] + inners[:1]][:-1]

    barrier = pltpu.get_barrier_semaphore()
    for p in peers:
        pl.semaphore_signal(barrier, inc=1, device_id={"ctx": p}, device_id_type=MESH)

    def remote(src, dst, ssem, rsem, p):
        pltpu.make_async_remote_copy(
            src_ref=src, dst_ref=dst, send_sem=ssem, recv_sem=rsem, device_id={"ctx": p}, device_id_type=MESH
        ).start()

    def arrived(ref, sem):
        pltpu.make_async_copy(ref, ref, sem).wait()

    def send_all(src_of, dst, ssem, rsem):
        pltpu.make_async_copy(src_of(me), dst.at[me], rsem).start()
        for p in peers:
            remote(src_of(p), dst.at[me], ssem, rsem, p)

    def put_block(b, q):
        toks = slice(q * LANES, (q + 1) * LANES)
        lanes = slice(b * LANES, (b + 1) * LANES)
        vt[q + 1, lanes, :] = vi[toks, lanes].astype(F32).T.astype(BF16)
        igt[q, lanes, :] = ig[toks, lanes].astype(F32).T

    last_in = (my_z >= n_z - n_z // 4) & (my_x == 1)

    def enter():
        pl.semaphore_wait(barrier, n_dev - 1)

        @pl.when(me < n_dev - 1)
        def _():
            remote(vi_any.at[pl.ds(tokens - LANES, LANES), :], halo, halo_sem.at[0], halo_sem.at[1], me + 1)

    pl.when(last_in)(enter)
    loads[0].wait()
    loads[1].wait()
    for q in range(q_count):
        for b in range(blocks):
            put_block(b, q)

    loads[2].wait()
    loads[3].wait()
    lane = lax.broadcasted_iota(jnp.int32, (LANES, LANES), 1)
    for b in range(blocks):
        lanes = slice(b * LANES, (b + 1) * LANES)
        high, low = halves(sf[:, lanes].T)
        upper = shf[0:LANES, :]
        freq = mm(high, upper) + mm(low, upper) + mm(high, shf[2 * LANES : 3 * LANES, :])
        f_re, f_im = freq[:, 0:LANES], freq[:, LANES:]
        taps[0, lanes, :] = f_re
        taps[1, lanes, :] = jnp.where(lane == 0, 0.0, f_im)
        taps[2, lanes, :] = jnp.where(lane == 0, f_im, f_re)

    loads[4].wait()
    for g in range(n_dev // 2):
        for q in range(q_count):
            fsend[g, pl.ds(q, 1), :] = lf[pl.ds(g, 1), q * LANES : (q + 1) * LANES]
    loads[5].wait()

    def short(q):
        for b in range(blocks):
            lanes = slice(b * LANES, (b + 1) * LANES)
            window = jnp.concatenate([vt[q, lanes, :], vt[q + 1, lanes, :]], axis=1)
            freq = mm(jnp.concatenate([window, window], axis=1), shf[...])
            re, im = freq[:, 0:LANES], freq[:, LANES:]
            f_re, f_zero, f_top = taps[0, lanes, :], taps[1, lanes, :], taps[2, lanes, :]
            prod = jnp.concatenate([re * f_re - im * f_zero, re * f_zero + im * f_top], axis=1)
            high, low = halves(prod)
            wide = mm(high, shi[...])
            keep[q, lanes, :] = igt[q, lanes, :] * (wide[:, 0:LANES] + wide[:, LANES:] + mm(low, shi[:, 0:LANES]))

    share = LANES // parts

    def pack(part):
        q = 2 * part
        top = peak(keep[q : q + 2].reshape(2 * chans, LANES))
        tsend[:, part * share : (part + 1) * share] = top[:, 0:share]
        first = encode(keep[q], top).reshape(n_dev, OWN, LANES)
        second = encode(keep[q + 1], top).reshape(n_dev, OWN, LANES)
        msend[part] = jnp.concatenate([first, second], axis=1).astype(BF16)

    for q in range(q_count - 1, 0, -1):
        short(q)
    for part in range(parts - 1, 0, -1):
        pack(part)

    pl.when(jnp.logical_not(last_in))(enter)

    def send_part(part):
        send_all(lambda p: msend.at[part, p], mrecv.at[part], ms_sem.at[part], mr_sem.at[part, my_half])

    my_pair = 2 * my_z + my_x
    for k in range(n_dev // 2):
        z, x = planes[k // 2], k % 2
        g = (z // 2) + wrap(my_x + 1 - x, 2)
        if k < n_dev // 2 - 1:
            remote(fsend.at[g], frecv.at[my_core, my_pair], fs_sem.at[0], fr_sem.at[0], 2 * g + my_core)
        else:
            pltpu.make_async_copy(fsend.at[my_pair], frecv.at[my_core, my_pair], fr_sem.at[0]).start()
    for part in range(parts - 1, 0, -1):
        send_part(part)

    @pl.when(me > 0)
    def _():
        pltpu.make_async_copy(halo, halo, halo_sem.at[1]).wait()

    for b in range(blocks):
        lanes = slice(b * LANES, (b + 1) * LANES)
        before = halo[:, lanes].astype(F32).T
        vt[0, lanes, :] = jnp.where(me > 0, before, 0.0).astype(BF16)
    short(0)
    pack(0)
    send_all(lambda p: tsend, trecv, ts_sem, tr_sem.at[my_half])
    send_part(0)
    arrived(frecv.at[my_core], fr_sem.at[0])
    remote(frecv.at[my_core], frecv.at[my_core], fs_sem.at[1], fr_sem.at[1], partner)

    for i in range(6, len(order)):
        loads[i].wait()
    for b in range(blocks):
        lanes = slice(b * LANES, (b + 1) * LANES)
        skipt[lanes, :] = jnp.broadcast_to(skip[:, lanes], (LANES, LANES)).T

    turn_re = turn[0:rows, :]
    turn_im = turn[rows:, :]

    def forward(block):
        high, low = halves(block)
        first = mm(colf[...], jnp.concatenate([high, low, high], axis=0))
        pieces = []
        for k in range(block.shape[1] // LANES):
            re = first[0:rows, k * LANES : (k + 1) * LANES]
            im = first[rows:, k * LANES : (k + 1) * LANES]
            pieces.append(jnp.concatenate([re * turn_re - im * turn_im, re * turn_im + im * turn_re], axis=1))
        return along(jnp.concatenate(pieces, axis=0), rowf[...])

    def backward(block):
        mid = along(block, rowi[...])
        reals, imags = [], []
        for c in range(OWN):
            re = mid[c * rows : (c + 1) * rows, 0:LANES]
            im = mid[c * rows : (c + 1) * rows, LANES:]
            reals.append(re * turn_re + im * turn_im)
            imags.append(im * turn_re - re * turn_im)
        high, low = halves(jnp.concatenate([jnp.concatenate(reals, axis=1), jnp.concatenate(imags, axis=1)], axis=0))
        return jnp.concatenate([high, low, high], axis=0)

    def times(spectra, which):
        h_re = spec[which, :, 0:LANES]
        h_im = spec[which, :, LANES:]
        out = []
        for c in range(OWN):
            re = spectra[c * rows : (c + 1) * rows, 0:LANES]
            im = spectra[c * rows : (c + 1) * rows, LANES:]
            out.append(jnp.concatenate([re * h_re - im * h_im, re * h_im + im * h_re], axis=1))
        return jnp.concatenate(out, axis=0)

    arrived(frecv.at[0], fr_sem.at[1])
    for s in range(n_dev):
        which, at = s // half_dev, s % half_dev
        fin[q_count * at : q_count * (at + 1), which * LANES : (which + 1) * LANES] = frecv[s % 2, s // 2]
    both = forward(fin[...]) * (1.0 / (rows * LANES))
    spec[0] = both[0:rows]
    spec[1] = both[rows:]

    def owned(half):
        span = pl.ds(half * half_dev, half_dev)
        got = []
        for part in range(parts):
            arrived(mrecv.at[part, span], mr_sem.at[part, half])
        arrived(trecv.at[span], tr_sem.at[half])
        tops = trecv[span].reshape(half_dev, LANES)
        for part in range(parts):
            one = tops
            if parts > 1:
                at = lax.broadcasted_iota(jnp.int32, (half_dev, LANES), 1) // share
                one = jnp.zeros_like(tops)
                for k in range(parts):
                    moved = pltpu.roll(tops, (k - part) * share % LANES, 1) if k != part else tops
                    one = jnp.where(at == k, moved, one)
            got.append(decode(mrecv[part, span].astype(F32), one.reshape(half_dev, 1, LANES)))
        xs[...] = jnp.concatenate(got, axis=1).reshape(rows * OWN, LANES)
        return jnp.concatenate([xs[pl.ds(c, rows, stride=OWN), :] for c in range(OWN)], axis=1)

    def give_back(half, result):
        top = peak(result)
        usend[half] = top
        wide = jnp.concatenate([top] * OWN, axis=1)
        code = encode(result, wide)
        for c in range(OWN):
            xs[pl.ds(c, rows, stride=OWN), :] = code[:, c * LANES : (c + 1) * LANES]
        rsend[half] = xs[...].reshape(half_dev, q_count * OWN, LANES).astype(BF16)
        for z in range(half_z):
            for i in inners[1:] + inners[:1]:
                at = z * INNER + i
                p = half * half_dev + at

                def away():
                    remote(rsend.at[half, at], rrecv.at[me], rs_sem, rr_sem, p)
                    remote(usend.at[half], urecv.at[me], us_sem, ur_sem, p)

                if i is not inners[0]:
                    away()
                    continue
                pl.when(my_z != half * half_z + z)(away)

                @pl.when(my_z == half * half_z + z)
                def _():
                    pltpu.make_async_copy(rsend.at[half, at], rrecv.at[me], rr_sem).start()
                    pltpu.make_async_copy(usend.at[half], urecv.at[me], ur_sem).start()

    spectra = forward(owned(0))
    ready[...] = backward(times(spectra, 0))
    give_back(0, mm(coli[0:rows, :], ready[...]))
    carry[...] = mm(coli[rows:, :], ready[...])
    cross[...] = times(spectra, 1)
    spectra = forward(owned(1))
    give_back(1, mm(coli[0:rows, :], backward(times(spectra, 0) + cross[...])) + carry[...])

    arrived(rrecv, rr_sem)
    arrived(urecv, ur_sem)
    for q in range(q_count):
        toks = slice(q * LANES, (q + 1) * LANES)
        code = rrecv[:, (q // 2) * 2 * OWN : (q // 2 + 1) * 2 * OWN, :].astype(F32)[:, (q % 2) * OWN : (q % 2 + 1) * OWN, :]
        total = decode(code, urecv[...]).reshape(chans, LANES) + skipt[...] * keep[q]
        for b in range(blocks):
            lanes = slice(b * LANES, (b + 1) * LANES)
            out[toks, lanes] = (og[toks, lanes].astype(F32) * total[lanes, :].T).astype(BF16)

    sent = pl.ds(0, n_dev - 1)

    @pl.when(me < n_dev - 1)
    def _():
        arrived(halo, halo_sem.at[0])

    arrived(frecv.at[0, pl.ds(0, n_dev // 2 - 1)], fs_sem.at[0])
    arrived(frecv.at[0], fs_sem.at[1])
    for part in range(parts):
        arrived(mrecv.at[part, sent], ms_sem.at[part])
    arrived(trecv.at[sent], ts_sem)
    arrived(rrecv.at[sent], rs_sem)
    arrived(urecv.at[sent], us_sem)


def local(n_z, output_gate, input_gate, value_input, short_filter, long_filter, skip_gain):
    n_dev = n_z * INNER
    tokens, chans = value_input.shape
    q_count = tokens // LANES
    parts = q_count // 2
    rows = n_dev * q_count // 2
    tabs = [jnp.asarray(t) for t in long_tables(rows) + short_tables()]
    operands = [output_gate, input_gate, value_input, short_filter, long_filter.T, skip_gain.reshape(1, chans)] + tabs
    dma = pltpu.SemaphoreType.DMA
    scratch = [pltpu.VMEM(x.shape, x.dtype) for x in operands]
    scratch += [
        pltpu.VMEM((LANES, chans), BF16),
        pltpu.VMEM((q_count + 1, chans, LANES), BF16),
        pltpu.VMEM((q_count, chans, LANES), F32),
        pltpu.VMEM((chans, LANES), F32),
        pltpu.VMEM((3, chans, LANES), F32),
        pltpu.VMEM((q_count, chans, LANES), F32),
        pltpu.VMEM((n_dev // 2, q_count, LANES), F32),
        pltpu.VMEM((2, n_dev // 2, q_count, LANES), F32),
        pltpu.VMEM((parts, n_dev, 2 * OWN, LANES), BF16),
        pltpu.VMEM((parts, n_dev, 2 * OWN, LANES), BF16),
        pltpu.VMEM((1, LANES), F32),
        pltpu.VMEM((n_dev, 1, LANES), F32),
        pltpu.VMEM((2, n_dev // 2, q_count * OWN, LANES), BF16),
        pltpu.VMEM((n_dev, q_count * OWN, LANES), BF16),
        pltpu.VMEM((2, 1, LANES), F32),
        pltpu.VMEM((n_dev, 1, LANES), F32),
        pltpu.VMEM((2, rows, 2 * LANES), F32),
        pltpu.VMEM((rows * OWN, LANES), F32),
        pltpu.VMEM((rows * OWN, 2 * LANES), F32),
        pltpu.VMEM((rows, OWN * LANES), F32),
        pltpu.VMEM((6 * rows, OWN * LANES), BF16),
        pltpu.VMEM((rows, 2 * LANES), F32),
        dma((len(operands),)), dma((2,)), dma((2,)), dma((2,)), dma((parts,)), dma((parts, 2)), dma, dma((2,)),
        dma, dma, dma, dma,
    ]
    return pl.pallas_call(
        functools.partial(kernel, n_z),
        out_shape=pltpu.VMEM((tokens, chans), BF16),
        in_specs=[pl.BlockSpec(memory_space=pl.ANY)] * len(operands),
        out_specs=pl.BlockSpec(memory_space=pltpu.VMEM),
        scratch_shapes=scratch,
        compiler_params=pltpu.CompilerParams(collective_id=0, has_side_effects=True, vmem_limit_bytes=60 << 20),
    )(*operands)


def solution(mesh):
    placed = (
        P("ctx", "ch"),
        P("ctx", "ch"),
        P("ctx", "ch"),
        P(None, "ch"),
        P("ctx", "ch"),
        P("ch"),
    )
    n_z = mesh.shape["ctx"] // INNER
    return jax.shard_map(
        functools.partial(local, n_z), mesh=mesh, in_specs=placed, out_specs=P("ctx", "ch"), check_vma=False
    )
```

```python
import functools
import math

import jax
import jax.numpy as jnp
import numpy as np
from jax import lax
from jax.experimental import pallas as pl
from jax.experimental.pallas import tpu as pltpu
from jax.sharding import PartitionSpec as P

LANES = 128
OWN = 8
INNER = 4
F32 = jnp.float32
BF16 = jnp.bfloat16
MESH = pl.DeviceIdType.MESH
KNEE = 64.0
SPAN = 120.0
POWER = 2 * SPAN / math.log2(1 + KNEE)


def split_np(table):
    table = table.astype(np.float32)
    high = table.astype(BF16)
    low = (table - high.astype(np.float32)).astype(BF16)
    return high, low


def long_tables(rows):
    length = rows * LANES
    n1 = np.arange(rows)
    n2 = np.arange(LANES)
    first = np.pi * n1[None, :] * LANES / (2 * length) - 2 * np.pi * ((n1[:, None] * n1[None, :]) % rows) / rows
    twist = np.pi * n2[None, :] / (2 * length) - 2 * np.pi * ((n1[:, None] * n2[None, :]) % length) / length
    second = -2 * np.pi * ((n2[:, None] * n2[None, :]) % LANES) / LANES
    hi, lo = split_np(np.concatenate([np.cos(first), np.sin(first)], 0))
    col_fwd = np.concatenate([hi, hi, lo], 1)
    cos1, sin1 = np.cos(first).T, np.sin(first).T
    hi, lo = split_np(np.block([[cos1, sin1], [-sin1, cos1]]))
    col_inv = np.concatenate([hi, hi, lo], 1)
    cos2, sin2 = np.cos(second), np.sin(second)
    row = np.block([[cos2, sin2], [-sin2, cos2]])
    hi, lo = split_np(row)
    row_fwd = np.concatenate([hi, hi, lo], 0)
    hi, lo = split_np(row.T)
    row_inv = np.concatenate([hi, hi, lo], 0)
    turn = np.concatenate([np.cos(twist), np.sin(twist)], 0).astype(np.float32)
    return col_fwd, col_inv, row_fwd, row_inv, turn


def short_tables():
    size = 2 * LANES
    n = np.arange(size)
    k = np.arange(LANES)
    angle = 2 * np.pi * ((n[:, None] * k[None, :]) % size) / size
    re, im = np.cos(angle), -np.sin(angle)
    im[:, 0] = np.where(n % 2 == 0, 1.0, -1.0)
    fwd = np.concatenate(split_np(np.concatenate([re, im], 1)), 0)
    weight = np.where(k == 0, 1.0, 2.0) / size
    back = np.concatenate([(re * weight).T, (im * weight).T], 0)[:, LANES:]
    inv = np.concatenate(split_np(back), 1)
    return fwd, inv


def mm(a, b):
    return jnp.dot(a, b, preferred_element_type=F32)


def halves(x):
    high = x.astype(BF16)
    return high, (x - high.astype(F32)).astype(BF16)


def peak(x):
    top = jnp.max(jnp.max(jnp.abs(x), axis=0, keepdims=True), axis=1, keepdims=True)
    return jnp.broadcast_to(jnp.maximum(top, 1e-30), (1, LANES))


def encode(x, top):
    size = jnp.exp2(POWER * jnp.log2(1.0 + jnp.abs(x) * (KNEE / top)) - SPAN)
    return jnp.where(x < 0, -size, size)


def decode(code, top):
    size = (jnp.exp2((jnp.log2(jnp.abs(code)) + SPAN) * (1.0 / POWER)) - 1.0) * (top * (1.0 / KNEE))
    return jnp.where(code < 0, -size, size)


def along(block, table):
    high, low = halves(block)
    return mm(jnp.concatenate([high, low, high], axis=1), table)


def kernel(
    n_z,
    og_any, ig_any, vi_any, sf_any, lf_any, skip_any, colf_any, coli_any, rowf_any, rowi_any, turn_any, shf_any, shi_any,
    out,
    og, ig, vi, sf, lf, skip, colf, coli, rowf, rowi, turn, shf, shi,
    halo, vt, igt, skipt, taps, keep, fsend, frecv, msend, mrecv, tsend, trecv, rsend, rrecv, usend, urecv,
    spec, xs, cross, carry, ready, fin,
    in_sem, halo_sem, fs_sem, fr_sem, ms_sem, mr_sem, ts_sem, tr_sem, rs_sem, rr_sem, us_sem, ur_sem,
):
    n_dev = n_z * INNER
    half_z = n_z // 2
    half_dev = n_dev // 2
    order = [
        (vi_any, vi), (ig_any, ig), (shf_any, shf), (sf_any, sf), (lf_any, lf), (shi_any, shi), (og_any, og), (skip_any, skip),
        (colf_any, colf), (coli_any, coli), (rowf_any, rowf), (rowi_any, rowi), (turn_any, turn),
    ]
    loads = [pltpu.make_async_copy(src, dst, in_sem.at[i]) for i, (src, dst) in enumerate(order)]
    for copy in loads:
        copy.start()

    def wrap(x, n):
        return jnp.where(x >= n, x - n, x)

    me = lax.axis_index("ctx")
    my_z = me // INNER
    my_in = me - my_z * INNER
    my_x = my_in // 2
    my_core = my_in - my_x * 2
    partner = me + 1 - 2 * my_core
    my_half = jnp.where(my_z >= half_z, 1, 0)
    tokens, chans = vi.shape
    q_count = tokens // LANES
    rows = half_dev * q_count
    blocks = chans // LANES
    parts = q_count // 2
    per_block = LANES // OWN

    inners = [my_in] + [wrap(my_in + r, INNER) for r in range(1, INNER)]
    turns = [n_z // 2]
    for d in range(n_z // 2 - 1, 0, -1):
        turns += [d, -d]
    turns += [0]
    ahead = {d: wrap(my_z + d + (n_z if d < 0 else 0), n_z) * INNER for d in turns}
    flip = {d: (-d if -d in ahead else d) for d in turns}
    planes = [jnp.where(my_core == 0, ahead[d], ahead[flip[d]]) for d in turns]
    peers = [z + i for z in planes for i in inners[1:] + inners[:1]][:-1]

    barrier = pltpu.get_barrier_semaphore()
    for p in peers:
        pl.semaphore_signal(barrier, inc=1, device_id={"ctx": p}, device_id_type=MESH)

    def remote(src, dst, ssem, rsem, p):
        pltpu.make_async_remote_copy(
            src_ref=src, dst_ref=dst, send_sem=ssem, recv_sem=rsem, device_id={"ctx": p}, device_id_type=MESH
        ).start()

    def arrived(ref, sem):
        pltpu.make_async_copy(ref, ref, sem).wait()

    def send_all(src_of, dst, ssem, rsem):
        pltpu.make_async_copy(src_of(me), dst.at[me], rsem).start()
        for p in peers:
            remote(src_of(p), dst.at[me], ssem, rsem, p)

    def put_block(b, q):
        toks = slice(q * LANES, (q + 1) * LANES)
        lanes = slice(b * LANES, (b + 1) * LANES)
        vt[q + 1, lanes, :] = vi[toks, lanes].astype(F32).T.astype(BF16)
        igt[q, lanes, :] = ig[toks, lanes].astype(F32).T

    last_in = (my_z >= n_z - n_z // 4) & (my_x == 1)

    def enter():
        pl.semaphore_wait(barrier, n_dev - 1)

        @pl.when(me < n_dev - 1)
        def _():
            remote(vi_any.at[pl.ds(tokens - LANES, LANES), :], halo, halo_sem.at[0], halo_sem.at[1], me + 1)

    pl.when(last_in)(enter)
    loads[0].wait()
    loads[1].wait()
    for q in range(q_count):
        for b in range(blocks):
            put_block(b, q)

    loads[2].wait()
    loads[3].wait()
    lane = lax.broadcasted_iota(jnp.int32, (LANES, LANES), 1)
    for b in range(blocks):
        lanes = slice(b * LANES, (b + 1) * LANES)
        high, low = halves(sf[:, lanes].T)
        upper = shf[0:LANES, :]
        freq = mm(high, upper) + mm(low, upper) + mm(high, shf[2 * LANES : 3 * LANES, :])
        f_re, f_im = freq[:, 0:LANES], freq[:, LANES:]
        taps[0, lanes, :] = f_re
        taps[1, lanes, :] = jnp.where(lane == 0, 0.0, f_im)
        taps[2, lanes, :] = jnp.where(lane == 0, f_im, f_re)

    loads[4].wait()
    for g in range(n_dev // 2):
        for q in range(q_count):
            fsend[g, pl.ds(q, 1), :] = lf[pl.ds(g, 1), q * LANES : (q + 1) * LANES]
    loads[5].wait()

    def short(q):
        for b in range(blocks):
            lanes = slice(b * LANES, (b + 1) * LANES)
            window = jnp.concatenate([vt[q, lanes, :], vt[q + 1, lanes, :]], axis=1)
            freq = mm(jnp.concatenate([window, window], axis=1), shf[...])
            re, im = freq[:, 0:LANES], freq[:, LANES:]
            f_re, f_zero, f_top = taps[0, lanes, :], taps[1, lanes, :], taps[2, lanes, :]
            prod = jnp.concatenate([re * f_re - im * f_zero, re * f_zero + im * f_top], axis=1)
            high, low = halves(prod)
            wide = mm(high, shi[...])
            keep[q, lanes, :] = igt[q, lanes, :] * (wide[:, 0:LANES] + wide[:, LANES:] + mm(low, shi[:, 0:LANES]))

    share = LANES // parts

    def pack(part):
        q = 2 * part
        top = peak(keep[q : q + 2].reshape(2 * chans, LANES))
        tsend[:, part * share : (part + 1) * share] = top[:, 0:share]
        first = encode(keep[q], top).reshape(n_dev, OWN, LANES)
        second = encode(keep[q + 1], top).reshape(n_dev, OWN, LANES)
        msend[part] = jnp.concatenate([first, second], axis=1).astype(BF16)

    for q in range(q_count - 1, 0, -1):
        short(q)
    for part in range(parts - 1, 0, -1):
        pack(part)

    pl.when(jnp.logical_not(last_in))(enter)

    def send_part(part):
        send_all(lambda p: msend.at[part, p], mrecv.at[part], ms_sem.at[part], mr_sem.at[part, my_half])

    my_pair = 2 * my_z + my_x
    for k in range(n_dev // 2):
        z, x = planes[k // 2], k % 2
        g = (z // 2) + wrap(my_x + 1 - x, 2)
        if k < n_dev // 2 - 1:
            remote(fsend.at[g], frecv.at[my_core, my_pair], fs_sem.at[0], fr_sem.at[0], 2 * g + my_core)
        else:
            pltpu.make_async_copy(fsend.at[my_pair], frecv.at[my_core, my_pair], fr_sem.at[0]).start()
    for part in range(parts - 1, 0, -1):
        send_part(part)

    @pl.when(me > 0)
    def _():
        pltpu.make_async_copy(halo, halo, halo_sem.at[1]).wait()

    for b in range(blocks):
        lanes = slice(b * LANES, (b + 1) * LANES)
        before = halo[:, lanes].astype(F32).T
        vt[0, lanes, :] = jnp.where(me > 0, before, 0.0).astype(BF16)
    short(0)
    pack(0)
    send_all(lambda p: tsend, trecv, ts_sem, tr_sem.at[my_half])
    send_part(0)
    arrived(frecv.at[my_core], fr_sem.at[0])
    remote(frecv.at[my_core], frecv.at[my_core], fs_sem.at[1], fr_sem.at[1], partner)

    for i in range(6, len(order)):
        loads[i].wait()
    for b in range(blocks):
        lanes = slice(b * LANES, (b + 1) * LANES)
        skipt[lanes, :] = jnp.broadcast_to(skip[:, lanes], (LANES, LANES)).T

    turn_re = turn[0:rows, :]
    turn_im = turn[rows:, :]

    def forward(block):
        high, low = halves(block)
        first = mm(colf[...], jnp.concatenate([high, low, high], axis=0))
        pieces = []
        for k in range(block.shape[1] // LANES):
            re = first[0:rows, k * LANES : (k + 1) * LANES]
            im = first[rows:, k * LANES : (k + 1) * LANES]
            pieces.append(jnp.concatenate([re * turn_re - im * turn_im, re * turn_im + im * turn_re], axis=1))
        return along(jnp.concatenate(pieces, axis=0), rowf[...])

    def backward(block):
        mid = along(block, rowi[...])
        reals, imags = [], []
        for c in range(OWN):
            re = mid[c * rows : (c + 1) * rows, 0:LANES]
            im = mid[c * rows : (c + 1) * rows, LANES:]
            reals.append(re * turn_re + im * turn_im)
            imags.append(im * turn_re - re * turn_im)
        high, low = halves(jnp.concatenate([jnp.concatenate(reals, axis=1), jnp.concatenate(imags, axis=1)], axis=0))
        return jnp.concatenate([high, low, high], axis=0)

    def times(spectra, which):
        h_re = spec[which, :, 0:LANES]
        h_im = spec[which, :, LANES:]
        out = []
        for c in range(OWN):
            re = spectra[c * rows : (c + 1) * rows, 0:LANES]
            im = spectra[c * rows : (c + 1) * rows, LANES:]
            out.append(jnp.concatenate([re * h_re - im * h_im, re * h_im + im * h_re], axis=1))
        return jnp.concatenate(out, axis=0)

    arrived(frecv.at[0], fr_sem.at[1])
    for s in range(n_dev):
        which, at = s // half_dev, s % half_dev
        fin[q_count * at : q_count * (at + 1), which * LANES : (which + 1) * LANES] = frecv[s % 2, s // 2]
    both = forward(fin[...]) * (1.0 / (rows * LANES))
    spec[0] = both[0:rows]
    spec[1] = both[rows:]

    def owned(half):
        span = pl.ds(half * half_dev, half_dev)
        got = []
        for part in range(parts):
            arrived(mrecv.at[part, span], mr_sem.at[part, half])
        arrived(trecv.at[span], tr_sem.at[half])
        tops = trecv[span].reshape(half_dev, LANES)
        for part in range(parts):
            one = tops
            if parts > 1:
                at = lax.broadcasted_iota(jnp.int32, (half_dev, LANES), 1) // share
                one = jnp.zeros_like(tops)
                for k in range(parts):
                    moved = pltpu.roll(tops, (k - part) * share % LANES, 1) if k != part else tops
                    one = jnp.where(at == k, moved, one)
            got.append(decode(mrecv[part, span].astype(F32), one.reshape(half_dev, 1, LANES)))
        xs[...] = jnp.concatenate(got, axis=1).reshape(rows * OWN, LANES)
        return jnp.concatenate([xs[pl.ds(c, rows, stride=OWN), :] for c in range(OWN)], axis=1)

    def give_back(half, result):
        top = peak(result)
        usend[half] = top
        wide = jnp.concatenate([top] * OWN, axis=1)
        code = encode(result, wide)
        for c in range(OWN):
            xs[pl.ds(c, rows, stride=OWN), :] = code[:, c * LANES : (c + 1) * LANES]
        rsend[half] = xs[...].reshape(half_dev, q_count * OWN, LANES).astype(BF16)
        for z in range(half_z):
            for i in inners[1:] + inners[:1]:
                at = z * INNER + i
                p = half * half_dev + at

                def away():
                    remote(rsend.at[half, at], rrecv.at[me], rs_sem, rr_sem, p)
                    remote(usend.at[half], urecv.at[me], us_sem, ur_sem, p)

                if i is not inners[0]:
                    away()
                    continue
                pl.when(my_z != half * half_z + z)(away)

                @pl.when(my_z == half * half_z + z)
                def _():
                    pltpu.make_async_copy(rsend.at[half, at], rrecv.at[me], rr_sem).start()
                    pltpu.make_async_copy(usend.at[half], urecv.at[me], ur_sem).start()

    spectra = forward(owned(0))
    ready[...] = backward(times(spectra, 0))
    give_back(0, mm(coli[0:rows, :], ready[...]))
    carry[...] = mm(coli[rows:, :], ready[...])
    cross[...] = times(spectra, 1)
    spectra = forward(owned(1))
    give_back(1, mm(coli[0:rows, :], backward(times(spectra, 0) + cross[...])) + carry[...])

    for q in range(q_count):
        keep[q] = skipt[...] * keep[q]
    arrived(rrecv, rr_sem)
    arrived(urecv, ur_sem)
    for q in range(q_count):
        toks = slice(q * LANES, (q + 1) * LANES)
        code = rrecv[:, (q // 2) * 2 * OWN : (q // 2 + 1) * 2 * OWN, :].astype(F32)[:, (q % 2) * OWN : (q % 2 + 1) * OWN, :]
        total = decode(code, urecv[...]).reshape(chans, LANES) + keep[q]
        for b in range(blocks):
            lanes = slice(b * LANES, (b + 1) * LANES)
            out[toks, lanes] = (og[toks, lanes].astype(F32) * total[lanes, :].T).astype(BF16)

    sent = pl.ds(0, n_dev - 1)

    @pl.when(me < n_dev - 1)
    def _():
        arrived(halo, halo_sem.at[0])

    arrived(frecv.at[0, pl.ds(0, n_dev // 2 - 1)], fs_sem.at[0])
    arrived(frecv.at[0], fs_sem.at[1])
    for part in range(parts):
        arrived(mrecv.at[part, sent], ms_sem.at[part])
    arrived(trecv.at[sent], ts_sem)
    arrived(rrecv.at[sent], rs_sem)
    arrived(urecv.at[sent], us_sem)


def local(n_z, output_gate, input_gate, value_input, short_filter, long_filter, skip_gain):
    n_dev = n_z * INNER
    tokens, chans = value_input.shape
    q_count = tokens // LANES
    parts = q_count // 2
    rows = n_dev * q_count // 2
    tabs = [jnp.asarray(t) for t in long_tables(rows) + short_tables()]
    operands = [output_gate, input_gate, value_input, short_filter, long_filter.T, skip_gain.reshape(1, chans)] + tabs
    dma = pltpu.SemaphoreType.DMA
    scratch = [pltpu.VMEM(x.shape, x.dtype) for x in operands]
    scratch += [
        pltpu.VMEM((LANES, chans), BF16),
        pltpu.VMEM((q_count + 1, chans, LANES), BF16),
        pltpu.VMEM((q_count, chans, LANES), F32),
        pltpu.VMEM((chans, LANES), F32),
        pltpu.VMEM((3, chans, LANES), F32),
        pltpu.VMEM((q_count, chans, LANES), F32),
        pltpu.VMEM((n_dev // 2, q_count, LANES), F32),
        pltpu.VMEM((2, n_dev // 2, q_count, LANES), F32),
        pltpu.VMEM((parts, n_dev, 2 * OWN, LANES), BF16),
        pltpu.VMEM((parts, n_dev, 2 * OWN, LANES), BF16),
        pltpu.VMEM((1, LANES), F32),
        pltpu.VMEM((n_dev, 1, LANES), F32),
        pltpu.VMEM((2, n_dev // 2, q_count * OWN, LANES), BF16),
        pltpu.VMEM((n_dev, q_count * OWN, LANES), BF16),
        pltpu.VMEM((2, 1, LANES), F32),
        pltpu.VMEM((n_dev, 1, LANES), F32),
        pltpu.VMEM((2, rows, 2 * LANES), F32),
        pltpu.VMEM((rows * OWN, LANES), F32),
        pltpu.VMEM((rows * OWN, 2 * LANES), F32),
        pltpu.VMEM((rows, OWN * LANES), F32),
        pltpu.VMEM((6 * rows, OWN * LANES), BF16),
        pltpu.VMEM((rows, 2 * LANES), F32),
        dma((len(operands),)), dma((2,)), dma((2,)), dma((2,)), dma((parts,)), dma((parts, 2)), dma, dma((2,)),
        dma, dma, dma, dma,
    ]
    return pl.pallas_call(
        functools.partial(kernel, n_z),
        out_shape=pltpu.VMEM((tokens, chans), BF16),
        in_specs=[pl.BlockSpec(memory_space=pl.ANY)] * len(operands),
        out_specs=pl.BlockSpec(memory_space=pltpu.VMEM),
        scratch_shapes=scratch,
        compiler_params=pltpu.CompilerParams(collective_id=0, has_side_effects=True, vmem_limit_bytes=60 << 20),
    )(*operands)


def solution(mesh):
    placed = (
        P("ctx", "ch"),
        P("ctx", "ch"),
        P("ctx", "ch"),
        P(None, "ch"),
        P("ctx", "ch"),
        P("ch"),
    )
    n_z = mesh.shape["ctx"] // INNER
    return jax.shard_map(
        functools.partial(local, n_z), mesh=mesh, in_specs=placed, out_specs=P("ctx", "ch"), check_vma=False
    )
```
